32 devices in a mesh: dp: 16 (over z, y, x), segment: 2 (over core).
Axes of the slice: x: 2, y: 2, z: 4, core: 2. Of those that a mesh axis runs over, the one named last changes fastest.
Arguments:
- latents: bfloat16 [16384, 640], P('dp'), may hold values from -6 to 6
- noise: bfloat16 [16384, 640], P('dp'), may hold values from -6 to 6
- timesteps: int32 [128], P('dp'), may hold values from 100 to 799
- reward_dir: float32 [640], replicated, may hold values from -6 to 6
- gain: float32 [2, 640], P('segment'), may hold values from 0.5 to 1.5
- time_scale: float32 [2, 640], P('segment'), may hold values from -6 to 6
- w_in: bfloat16 [2, 640, 640], P('segment', 'dp'), may hold values from -0.25 to 0.25
- w_out: bfloat16 [2, 640, 640], P('segment', 'dp'), may hold values from -0.25 to 0.25
Outputs:
- weight_grads: float32 [2, 640, 1280], P('segment', 'dp')
The draws below stay inside these ranges and needn't reach their ends.
All inputs are finite; a program needn't handle non-finite values.
Results may differ from the reference program's by a relative error of at most 0.0004.
Values may be sent and summed in bfloat16 or wider, within the bound.
A program may use at most 64 MiB of HBM per device.

```python
import math
import jax
import jax.numpy as jnp
from jax import lax

C = 640
GROUPS = 32
NSTEPS = 1000
STRIDE = 20
MICRO = 8
ROWS_MB = 128
SEGMENTS = 2
IMAGES = 128
ROWS = 16384
N_DP = 16
N_SEGMENT = 2


def plant(array, stream_key, smallest, largest):
    longest = array.shape.index(max(array.shape))
    spots = []
    for shift in (0, 1):
        where = [jax.random.randint(jax.random.fold_in(stream_key, axis), (), 0, length) for axis, length in enumerate(array.shape)]
        where[longest] = (where[longest] + shift) % array.shape[longest]
        spots.append(tuple(where))
    return array.at[spots[0]].set(smallest).at[spots[1]].set(largest)


def raised(values, own_key, source, target, blocks, factor):
    def block_of(position):
        return (jnp.arange(values.shape[position]) // (values.shape[position] // blocks)).reshape((-1,) + (1,) * (values.ndim - 1 - position))

    near = jax.random.permutation(own_key, blocks)[block_of(target)]
    other_side = (block_of(target) + blocks // 2) % blocks
    return jnp.where((block_of(source) == near) | (block_of(source) == other_side), factor * values, values)


def level_of(own_key, shape, shards, low, high):
    level, own = 1.0, jax.random.fold_in(own_key, 6)
    for dim, blocks in shards:
        draws = jnp.exp(jax.random.uniform(jax.random.fold_in(own, dim), (blocks,), jnp.float32, low / len(shards), high / len(shards)))
        level = level * jnp.repeat(draws, shape[dim] // blocks).reshape([-1 if axis == dim else 1 for axis in range(len(shape))])
    return level


def scatter_about(rng, shape, spread, bound, pieces=(), kind=jnp.bfloat16):
    values = jax.random.normal(rng, shape, jnp.float32) * spread
    if len(pieces) > 0:
        values = level_of(rng, shape, pieces, -0.22, 0.18) * values
    return jnp.clip(values, min=-bound, max=bound).astype(kind)


def gaussian_with(key, extent, width, most, split, heavy, held_as=jnp.bfloat16):
    drawn = width * jax.random.normal(key, extent, jnp.float32)
    if split:
        drawn = drawn * level_of(key, extent, split, -0.22, 0.18)
    return jnp.clip(raised(drawn, jax.random.fold_in(key, 3), *heavy), -most, most).astype(held_as)


def setup_inputs(seed: int = 0) -> dict:
    arg_keys = jax.random.split(jax.random.key(seed), 9)
    latents = gaussian_with(arg_keys[0], (ROWS, C), 1.0, 6.0, ((0, 16),), (0, 1, 16, 2.0))
    noise = scatter_about(arg_keys[1], (ROWS, C), 1.0, 6.0, ((0, 16),))
    timesteps = plant(jax.random.randint(arg_keys[2], (IMAGES,), 100, 800), jax.random.fold_in(arg_keys[2], 1), 100, 799).astype(jnp.int32)
    reward_dir = scatter_about(arg_keys[3], (C,), 1.0, 6.0, (), jnp.float32)
    gain = jnp.clip(0.5 + 1.0 * jax.random.uniform(arg_keys[4], (SEGMENTS, C), jnp.float32) ** level_of(arg_keys[4], (SEGMENTS, C), ((0, 2),), -0.2, 0.2), 0.5, 1.5)
    time_scale = scatter_about(arg_keys[5], (SEGMENTS, C), 1.0, 6.0, ((0, 2),), jnp.float32)
    w_in = scatter_about(arg_keys[6], (SEGMENTS, C, C), C ** -0.5, 0.25, ((0, 2), (1, 16)))
    w_out = scatter_about(arg_keys[7], (SEGMENTS, C, C), C ** -0.5, 0.25, ((0, 2), (1, 16)))
    return {"latents": latents, "noise": noise, "timesteps": timesteps, "reward_dir": reward_dir, "gain": gain, "time_scale": time_scale, "w_in": w_in, "w_out": w_out}


EPS = 1e-05

def group_norm(state_f32, group_count):
    channels = state_f32.shape[1]
    per_group = channels // group_count
    col_mean = lax.optimization_barrier(jnp.mean(state_f32, axis=0))
    group_mean = jnp.repeat(lax.optimization_barrier(jnp.mean(col_mean.reshape(group_count, per_group), axis=1)), per_group)
    centered = state_f32 - group_mean
    sq_mean = lax.optimization_barrier(jnp.mean(centered * centered, axis=0))
    variance = jnp.repeat(lax.optimization_barrier(jnp.mean(sq_mean.reshape(group_count, per_group), axis=1)), per_group)
    return centered * lax.rsqrt(variance + EPS)

def time_embed(timestep, channels):
    half_width = channels // 2
    frequencies = jnp.exp(-math.log(10000.0) * jnp.arange(half_width).astype(jnp.float32) / half_width)
    phases = timestep.astype(jnp.float32) * frequencies
    return jnp.concatenate([jnp.sin(phases), jnp.cos(phases)])

def alpha_bar(timestep):
    value = ((timestep.astype(jnp.float32) + 1.0) / NSTEPS + 0.008) / 1.008 * (math.pi / 2.0)
    return jnp.cos(value) ** 2

def contract_rows(left, right):
    return lax.dot_general(left, right, (((0,), (0,)), ((), ())), preferred_element_type=jnp.float32)

def contract_cols(left, right):
    return lax.dot_general(left, right, (((1,), (1,)), ((), ())), preferred_element_type=jnp.float32)

def block_forward(hidden, gain_row, temb, first, second):
    state_f32 = hidden.astype(jnp.float32)
    normed = (group_norm(state_f32, GROUPS) * gain_row).astype(jnp.bfloat16)
    preact = jnp.dot(normed, first, preferred_element_type=jnp.float32) + temb
    activation = jax.nn.silu(preact).astype(jnp.bfloat16)
    result = (state_f32 + jnp.dot(activation, second, preferred_element_type=jnp.float32)).astype(jnp.bfloat16)
    return (result, normed, preact, activation)

def block_backward(hidden, gain_row, preact, cotangent, first, second):
    grad_act = contract_cols(cotangent, second)
    gate_value = jax.nn.sigmoid(preact)
    grad_pre = (grad_act * gate_value * (1.0 + preact * (1.0 - gate_value))).astype(jnp.bfloat16)
    grad_norm = contract_cols(grad_pre, first)
    _, pullback = jax.vjp(lambda values: group_norm(values, GROUPS), hidden.astype(jnp.float32))
    new_cot = (cotangent.astype(jnp.float32) + pullback(grad_norm * gain_row)[0]).astype(jnp.bfloat16)
    return (new_cot, grad_pre)

def weight_term(normed, grad_pre, activation, cotangent):
    return jnp.concatenate([contract_rows(normed, grad_pre), contract_rows(activation, cotangent)], axis=1)

def sample_head(hidden, latent, noise_block, timestep, reward_dir, loss_scale):
    ab_now = alpha_bar(timestep)
    ab_prev = alpha_bar(timestep - STRIDE)
    coef_a = jnp.sqrt(ab_now)
    coef_b = jnp.sqrt(1.0 - ab_now)
    coef_p = jnp.sqrt(ab_prev)
    coef_q = jnp.sqrt(0.75 * (1.0 - ab_prev))
    coef_r = 0.5 * jnp.sqrt(1.0 - ab_prev)
    noise_pred, pullback = jax.vjp(lambda values: group_norm(values, GROUPS), hidden.astype(jnp.float32))
    current = latent.astype(jnp.float32)
    previous = coef_p * (current - coef_b * noise_pred) / coef_a + coef_q * noise_pred + coef_r * noise_block.astype(jnp.float32)
    squashed = jnp.tanh(previous)
    grad_pred = (coef_q - coef_p * coef_b / coef_a) * reward_dir * (1.0 - squashed * squashed) * loss_scale
    return pullback(grad_pred)[0].astype(jnp.bfloat16)

def reference(latents, noise, timesteps, reward_dir, gain, time_scale, w_in, w_out):
    image_count = N_DP * MICRO
    latent_blocks = latents.reshape(image_count, ROWS_MB, C)
    noise_blocks = noise.reshape(image_count, ROWS_MB, C)
    loss_scale = 1.0 / math.sqrt(N_DP * MICRO * ROWS_MB)

    def per_image(grad_total, item):
        latent, noise_block, timestep = item
        embed = time_embed(timestep, C)
        hidden = latent
        inputs = []
        for section in range(N_SEGMENT):
            inputs.append(hidden)
            hidden = block_forward(hidden, gain[section], time_scale[section] * embed, w_in[section], w_out[section])[0]
        cotangent = sample_head(hidden, latent, noise_block, timestep, reward_dir, loss_scale)
        terms = [None] * N_SEGMENT
        for section in range(N_SEGMENT - 1, -1, -1):
            _, normed, preact, activation = block_forward(inputs[section], gain[section], time_scale[section] * embed, w_in[section], w_out[section])
            new_cot, grad_pre = block_backward(inputs[section], gain[section], preact, cotangent, w_in[section], w_out[section])
            terms[section] = weight_term(normed, grad_pre, activation, cotangent)
            cotangent = new_cot
        return (grad_total + jnp.stack(terms), None)
    grad_total, _ = lax.scan(per_image, jnp.zeros((N_SEGMENT, C, 2 * C), jnp.float32), (latent_blocks, noise_blocks, timesteps))
    return grad_total
```

```python
import functools
import math

import jax
import jax.numpy as jnp
from jax import lax
from jax.experimental import pallas as pl
from jax.experimental.pallas import tpu as pltpu
from jax.sharding import PartitionSpec as P

GROUPS = 32
NSTEPS = 1000
STRIDE = 20
LIMIT = 32760.0
TINY = 1e-30


EPS = 1e-05


def passed_along(shard, axis, by):
    length = lax.axis_size(axis)
    pairs = [(i, i + by) for i in range(length) if 0 <= i + by < length]
    return lax.ppermute(shard, axis, pairs)


def group_norm(state_f32, group_count):
    channels = state_f32.shape[1]
    per_group = channels // group_count
    col_mean = jnp.mean(state_f32, axis=0)
    group_mean = jnp.repeat(jnp.mean(col_mean.reshape(group_count, per_group), axis=1), per_group)
    centered = state_f32 - group_mean
    sq_mean = jnp.mean(centered * centered, axis=0)
    variance = jnp.repeat(jnp.mean(sq_mean.reshape(group_count, per_group), axis=1), per_group)
    return centered * lax.rsqrt(variance + EPS)


def time_embed(timestep, channels):
    half_width = channels // 2
    frequencies = jnp.exp(
        -math.log(10000.0) * jnp.arange(half_width).astype(jnp.float32) / half_width
    )
    phases = timestep.astype(jnp.float32) * frequencies
    return jnp.concatenate([jnp.sin(phases), jnp.cos(phases)])


def alpha_bar(timestep):
    value = ((timestep.astype(jnp.float32) + 1.0) / NSTEPS + 0.008) / 1.008 * (math.pi / 2.0)
    return jnp.cos(value) ** 2


def contract_rows(left, right):
    return lax.dot_general(
        left, right, (((0,), (0,)), ((), ())), preferred_element_type=jnp.float32
    )


def contract_cols(left, right):
    return lax.dot_general(
        left, right, (((1,), (1,)), ((), ())), preferred_element_type=jnp.float32
    )


def block_forward(hidden, gain_row, temb, first, second):
    state_f32 = hidden.astype(jnp.float32)
    normed = (group_norm(state_f32, GROUPS) * gain_row).astype(jnp.bfloat16)
    preact = jnp.dot(normed, first, preferred_element_type=jnp.float32) + temb
    activation = jax.nn.silu(preact).astype(jnp.bfloat16)
    result = (state_f32 + jnp.dot(activation, second, preferred_element_type=jnp.float32)).astype(
        jnp.bfloat16
    )
    return (result, normed, preact, activation)


def block_backward(hidden, gain_row, preact, cotangent, first, second):
    grad_act = contract_cols(cotangent, second)
    gate_value = jax.nn.sigmoid(preact)
    grad_pre = (grad_act * gate_value * (1.0 + preact * (1.0 - gate_value))).astype(jnp.bfloat16)
    grad_norm = contract_cols(grad_pre, first)
    _, pullback = jax.vjp(lambda values: group_norm(values, GROUPS), hidden.astype(jnp.float32))
    new_cot = (cotangent.astype(jnp.float32) + pullback(grad_norm * gain_row)[0]).astype(
        jnp.bfloat16
    )
    return (new_cot, grad_pre)


def weight_term(normed, grad_pre, activation, cotangent):
    return jnp.concatenate(
        [contract_rows(normed, grad_pre), contract_rows(activation, cotangent)], axis=1
    )


def sample_head(hidden, latent, noise_block, timestep, reward_dir, loss_scale):
    ab_now = alpha_bar(timestep)
    ab_prev = alpha_bar(timestep - STRIDE)
    coef_a = jnp.sqrt(ab_now)
    coef_b = jnp.sqrt(1.0 - ab_now)
    coef_p = jnp.sqrt(ab_prev)
    coef_q = jnp.sqrt(0.75 * (1.0 - ab_prev))
    coef_r = 0.5 * jnp.sqrt(1.0 - ab_prev)
    noise_pred, pullback = jax.vjp(
        lambda values: group_norm(values, GROUPS), hidden.astype(jnp.float32)
    )
    current = latent.astype(jnp.float32)
    previous = (
        coef_p * (current - coef_b * noise_pred) / coef_a
        + coef_q * noise_pred
        + coef_r * noise_block.astype(jnp.float32)
    )
    squashed = jnp.tanh(previous)
    grad_pred = (
        (coef_q - coef_p * coef_b / coef_a) * reward_dir * (1.0 - squashed * squashed) * loss_scale
    )
    return pullback(grad_pred)[0].astype(jnp.bfloat16)


def put_slot(buffer, value, slot_index):
    return lax.dynamic_update_index_in_dim(buffer, value, slot_index, 0)


def body(latents, noise, timesteps, reward_dir, gain, time_scale, w_in, w_out):
    segments = lax.axis_size("segment")
    segment_index = lax.axis_index("segment")
    last_segment = segments - 1
    micro_count = timesteps.shape[0]
    crop_rows = latents.shape[0] // micro_count
    channels = latents.shape[1]
    loss_scale = 1.0 / math.sqrt(lax.axis_size("dp") * latents.shape[0])
    tick_count = micro_count + segments - 1
    whole_in, whole_out = (
        lax.all_gather(w_in, "dp", axis=1, tiled=True),
        lax.all_gather(w_out, "dp", axis=1, tiled=True),
    )
    first = whole_in[0]
    second = whole_out[0]
    gain_row = gain[0]
    latent_blocks = latents.reshape(micro_count, crop_rows, channels)
    noise_blocks = noise.reshape(micro_count, crop_rows, channels)
    embeds = jax.vmap(lambda values: time_embed(values, channels))(timesteps) * time_scale[0]
    blank = jnp.zeros((crop_rows, channels), jnp.bfloat16)
    blank_stack = jnp.zeros((micro_count, crop_rows, channels), jnp.bfloat16)
    stored = ()

    def forward_tick(tick_index, state_carry):
        incoming, inputs, head_cots, kept = state_carry
        micro_index = tick_index - segment_index
        active = (micro_index >= 0) & (micro_index < micro_count)
        slot_index = jnp.clip(micro_index, 0, micro_count - 1)
        fresh_input = latent_blocks[slot_index]
        hidden = jnp.where(segment_index == 0, fresh_input, incoming)

        def forward_compute(buffers):
            inputs, head_cots, kept = buffers
            result, normed, preact, activation = block_forward(
                hidden, gain_row, embeds[slot_index], first, second
            )
            inputs = put_slot(inputs, hidden, slot_index)
            head_cot = lax.cond(
                segment_index == last_segment,
                lambda: sample_head(
                    result,
                    fresh_input,
                    noise_blocks[slot_index],
                    timesteps[slot_index],
                    reward_dir,
                    loss_scale,
                ),
                lambda: blank,
            )
            head_cots = put_slot(head_cots, head_cot, slot_index)
            return (result, inputs, head_cots, kept)

        def forward_skipped(buffers):
            return (blank, buffers[0], buffers[1], buffers[2])

        result, inputs, head_cots, kept = lax.cond(
            active, forward_compute, forward_skipped, (inputs, head_cots, kept)
        )
        incoming = passed_along(result, "segment", 1)
        return (incoming, inputs, head_cots, kept)

    _, inputs, head_cots, kept = lax.fori_loop(
        0, tick_count, forward_tick, (blank, blank_stack, blank_stack, stored)
    )
    grad_start = ()
    records = (blank_stack, blank_stack, blank_stack, blank_stack)

    def backward_tick(tick_index, state_carry):
        incoming, grad_sum, records = state_carry
        micro_index = tick_index - (last_segment - segment_index)
        active = (micro_index >= 0) & (micro_index < micro_count)
        slot_index = jnp.clip(micro_index, 0, micro_count - 1)
        cotangent = jnp.where(segment_index == last_segment, head_cots[slot_index], incoming)

        def backward_compute(buffers):
            grad_sum, records = buffers
            hidden = inputs[slot_index]
            _, normed, preact, activation = block_forward(
                hidden, gain_row, embeds[slot_index], first, second
            )
            new_cot, grad_pre = block_backward(hidden, gain_row, preact, cotangent, first, second)
            records = (
                put_slot(records[0], normed, slot_index),
                put_slot(records[1], grad_pre, slot_index),
                put_slot(records[2], activation, slot_index),
                put_slot(records[3], cotangent, slot_index),
            )
            return (new_cot, grad_sum, records)

        def backward_skipped(buffers):
            return (blank, buffers[0], buffers[1])

        result, grad_sum, records = lax.cond(
            active, backward_compute, backward_skipped, (grad_sum, records)
        )
        incoming = passed_along(result, "segment", -1)
        return (incoming, grad_sum, records)

    _, grad_sum, records = lax.fori_loop(0, tick_count, backward_tick, (blank, grad_start, records))
    flat = [buffer.reshape(micro_count * crop_rows, channels) for buffer in records]
    full_terms = weight_term(flat[0], flat[1], flat[2], flat[3])
    grad_rows = lax.psum_scatter(full_terms, "dp", scatter_dimension=0, tiled=True)
    return grad_rows[None]


def split_rows(values):
    high = values.astype(jnp.bfloat16).astype(jnp.float32)
    rest = values - high
    middle = rest.astype(jnp.bfloat16).astype(jnp.float32)
    low = rest - middle
    return jnp.concatenate([high, middle, low], axis=0).astype(jnp.bfloat16)


def encode(block, code_ref, size_ref):
    top = jnp.maximum(jnp.max(jnp.abs(block), axis=0, keepdims=True), TINY)
    size_ref[...] = top * (1.0 / LIMIT)
    code_ref[...] = jnp.round(block * (LIMIT / top)).astype(jnp.int32).astype(jnp.int16)


def decode(code_ref, size_ref):
    return code_ref[...].astype(jnp.int32).astype(jnp.float32) * size_ref[...]


def step_kernel(
    shape,
    win_ref,
    wout_ref,
    gain_ref,
    time_ref,
    latent_ref,
    noise_ref,
    times_ref,
    reward_ref,
    out_ref,
    embed_ref,
    coef_ref,
    wbuf,
    pbuf,
    weights,
    states,
    noises,
    normed,
    slopes,
    acts,
    cots,
    gradpre,
    means,
    scales,
    sums,
    spread,
    gather_mat,
    scatter_mat,
    grads,
    code_a,
    code_b,
    code_z,
    size_a,
    size_b,
    size_z,
    in_a,
    in_b,
    in_z,
    insize_a,
    insize_b,
    insize_z,
    send_sem,
    recv_sem,
    local_sem,
):
    dp, depth, shard, channels, images, rows, loss_scale = shape
    total_rows = images * rows
    me = lax.axis_index("dp")
    core = lax.axis_index("segment")
    other = 1 - core
    col = lax.rem(me, 4)
    z = me // 4
    qx = col + 1 - 2 * lax.rem(col, 2)
    qy = lax.rem(col + 2, 4)
    qd = 3 - col
    x_dev = (z * 4 + qx, core)
    y_dev = (z * 4 + qy, core)
    partner = (me, other)

    def flipped(j):
        place = z
        bit = 1
        while bit < depth:
            if j & bit:
                place = place + bit * (1 - 2 * lax.rem(z // bit, 2))
            bit *= 2
        return place

    zj = [flipped(j) for j in range(depth)]
    z_dev = [(zj[j] * 4 + col, core) for j in range(depth)]
    far = list(range(1, depth))
    early = list(range(depth // 2))
    late = list(range(depth // 2, depth))
    count = [0]
    sent = []

    def reserve(src, dst, device):
        k = count[0]
        count[0] += 1
        copy = pltpu.make_async_remote_copy(
            src_ref=src,
            dst_ref=dst,
            send_sem=send_sem.at[k],
            recv_sem=recv_sem.at[k],
            device_id=device,
            device_id_type=pl.DeviceIdType.MESH,
        )
        sent.append(copy)
        return copy

    base = pl.multiple_of(core * total_rows, total_rows)
    locals_ = [
        pltpu.make_async_copy(source, target, local_sem.at[k])
        for k, (source, target) in enumerate(
            (
                (win_ref.at[0], wbuf.at[core, 0, col, z]),
                (wout_ref.at[0], wbuf.at[core, 1, col, z]),
                (gain_ref, pbuf.at[core, 0]),
                (time_ref, pbuf.at[core, 1]),
                (latent_ref.at[pl.ds(base, total_rows)], states.at[0]),
                (noise_ref.at[pl.ds(base, total_rows)], noises),
            )
        )
    ]
    for copy in locals_:
        copy.start()

    barrier = pltpu.get_barrier_semaphore()
    friends = [x_dev, y_dev, partner] + z_dev[1:]
    for device in friends:
        pl.semaphore_signal(
            barrier, inc=1, device_id=device, device_id_type=pl.DeviceIdType.MESH
        )
    ch = lax.broadcasted_iota(jnp.int32, gather_mat.shape, 0)
    gr = lax.broadcasted_iota(jnp.int32, gather_mat.shape, 1) * (channels // GROUPS)
    inside = (ch >= gr) & (ch < gr + channels // GROUPS)
    gather_mat[...] = jnp.where(inside, 1.0, 0.0).astype(jnp.bfloat16)
    ch = lax.broadcasted_iota(jnp.int32, scatter_mat.shape, 1)
    gr = lax.broadcasted_iota(jnp.int32, scatter_mat.shape, 0) * (channels // GROUPS)
    inside = (ch >= gr) & (ch < gr + channels // GROUPS)
    scatter_mat[...] = jnp.where(inside, 1.0, 0.0).astype(jnp.bfloat16)
    sums[...] = jnp.zeros_like(sums)
    for copy in locals_[:4]:
        copy.wait()
    pl.semaphore_wait(barrier, len(friends))

    def piece(section, q, j):
        return wbuf.at[section, core, q, zj[j]]

    swap = [
        reserve(wbuf.at[core, kind, col, z], wbuf.at[core, kind, col, z], partner)
        for kind in (0, 1)
    ]
    tunes = [
        reserve(gain_ref, pbuf.at[core, 0], partner),
        reserve(time_ref, pbuf.at[core, 1], partner),
    ]
    to_x, to_y, to_z, to_core, to_diag, blocks = {}, {}, {}, {}, {}, {}
    for section in range(2):
        for j in range(depth):
            here = piece(section, col, j)
            to_x[section, j] = reserve(here, here, x_dev)
            to_y[section, j] = reserve(here, here, y_dev)
            if j > 0:
                to_core[section, j] = reserve(here, here, partner)
                own = piece(section, col, 0)
                to_z[section, j] = reserve(own, own, z_dev[j])
            q, device = (qx, y_dev) if j in early else (qy, x_dev)
            passed = piece(section, q, j)
            to_diag[section, j] = reserve(passed, passed, device)
        for q, name in ((qx, "x"), (qy, "y"), (qd, "d")):
            whole = wbuf.at[section, core, q]
            blocks[section, name] = reserve(whole, whole, partner)

    def send_own(section):
        to_x[section, 0].start()
        to_y[section, 0].start()
        for j in far:
            to_z[section, j].start()

    def take_swap():
        for copy in swap:
            copy.wait_recv()

    for copy in swap:
        copy.start()
    for mine in range(2):

        @pl.when(core == mine)
        def _(mine=mine):
            send_own(mine)

    take_swap()
    for mine in range(2):

        @pl.when(core == mine)
        def _(mine=mine):
            send_own(1 - mine)

    for copy in tunes:
        copy.start()

    def pass_line(section, steps):
        for j in steps:
            to_z[section, j].wait_recv()
            to_x[section, j].start()
            to_y[section, j].start()
            to_core[section, j].start()

    def pass_diag(section, steps):
        for j in steps:
            (to_x if j in early else to_y)[section, j].wait_recv()
            to_diag[section, j].start()

    def pass_sides(section):
        for j in late:
            to_x[section, j].wait_recv()
        blocks[section, "x"].start()
        for j in early:
            to_y[section, j].wait_recv()
        blocks[section, "y"].start()

    def pass_corner(section):
        for j in range(depth):
            to_diag[section, j].wait_recv()
        blocks[section, "d"].start()

    def arrived(section):
        for j in far:
            to_core[section, j].wait_recv()
        for name in ("x", "y", "d"):
            blocks[section, name].wait_recv()

    def column(stacked):
        line = lax.broadcasted_iota(jnp.int32, stacked.shape, 0)
        values = jnp.zeros(stacked.shape, jnp.float32)
        for i in range(images):
            values = jnp.where(
                line == i, times_ref[core * images + i].astype(jnp.float32), values
            )
        return values

    half_width = channels // 2
    lane = lax.broadcasted_iota(jnp.int32, embed_ref.shape, 1)
    k_index = jnp.where(lane < half_width, lane, lane - half_width).astype(jnp.float32)
    phases = column(embed_ref) * jnp.exp(-math.log(10000.0) * k_index / half_width)
    embed_ref[...] = jnp.where(lane < half_width, jnp.sin(phases), jnp.cos(phases))
    now = column(coef_ref.at[0])
    ab_now, ab_prev = alpha_bar(now), alpha_bar(now - STRIDE)
    coef_a, coef_b = jnp.sqrt(ab_now), jnp.sqrt(1.0 - ab_now)
    coef_p, coef_q = jnp.sqrt(ab_prev), jnp.sqrt(0.75 * (1.0 - ab_prev))
    coef_ref[0] = coef_p / coef_a
    coef_ref[1] = coef_q - coef_p * coef_b / coef_a
    coef_ref[2] = 0.5 * jnp.sqrt(1.0 - ab_prev)

    def group_means(values):
        parts = jnp.dot(
            split_rows(values), gather_mat[...], preferred_element_type=jnp.float32
        )
        lines = values.shape[0]
        total = parts[:lines] + parts[lines : 2 * lines] + parts[2 * lines :]
        total = total * (1.0 / (rows * (channels // GROUPS)))
        parts = jnp.dot(
            split_rows(total), scatter_mat[...], preferred_element_type=jnp.float32
        )
        return parts[:lines] + parts[lines : 2 * lines] + parts[2 * lines :]

    def statistics(stage):
        def mean_body(i, carry):
            block = states[stage, pl.ds(i * rows, rows), :].astype(jnp.float32)
            sums[pl.ds(i, 1), :] = jnp.sum(block, axis=0, keepdims=True)
            return carry

        lax.fori_loop(0, images, mean_body, 0)
        means[stage] = group_means(sums[...])

        def square_body(i, carry):
            block = states[stage, pl.ds(i * rows, rows), :].astype(jnp.float32)
            centered = block - means[stage, pl.ds(i, 1), :]
            sums[pl.ds(i, 1), :] = jnp.sum(centered * centered, axis=0, keepdims=True)
            return carry

        lax.fori_loop(0, images, square_body, 0)
        scales[stage] = lax.rsqrt(group_means(sums[...]) + EPS)

    def unit(stage, i):
        block = states[stage, pl.ds(i * rows, rows), :].astype(jnp.float32)
        return (block - means[stage, pl.ds(i, 1), :]) * scales[stage, pl.ds(i, 1), :]

    def normalize(section):
        statistics(section)
        gain_row = pbuf[section, 0]

        def norm_body(i, carry):
            where = pl.ds(pl.multiple_of(i * rows, rows), rows)
            normed[section, 0, where, :] = (unit(section, i) * gain_row).astype(jnp.bfloat16)
            return carry

        lax.fori_loop(0, images, norm_body, 0)

    def lay_out(section):
        for kind in range(2):
            for pair in range(dp // 2):
                q, zz = (2 * pair) % 4, pair // 2
                both = jnp.concatenate(
                    [
                        wbuf[section, kind, q, zz].astype(jnp.float32),
                        wbuf[section, kind, q + 1, zz].astype(jnp.float32),
                    ],
                    axis=0,
                )
                weights[section, kind, 2 * pair * shard : 2 * (pair + 1) * shard, :] = (
                    both.astype(jnp.bfloat16)
                )

    joint = 2 if images % 2 == 0 else 1
    groups = images // joint

    def forward(section, start, stop):
        time_row = pbuf[section, 1]

        def forward_body(g, carry):
            span = pl.ds(pl.multiple_of(g * joint * rows, rows), joint * rows)
            product = jnp.dot(
                normed[section, 0, span, :],
                weights[section, 0],
                preferred_element_type=jnp.float32,
            )
            for j in range(joint):
                i = g * joint + j
                where = pl.ds(pl.multiple_of(i * rows, rows), rows)
                preact = product[j * rows : (j + 1) * rows] + time_row * embed_ref[pl.ds(i, 1), :]
                gate = jax.nn.sigmoid(preact)
                acts[section, 0, where, :] = (preact * gate).astype(jnp.bfloat16)
                slopes[section, where, :] = gate * (1.0 + preact * (1.0 - gate))
            product = jnp.dot(
                acts[section, 0, span, :],
                weights[section, 1],
                preferred_element_type=jnp.float32,
            )
            states[section + 1, span, :] = (
                states[section, span, :].astype(jnp.float32) + product
            ).astype(jnp.bfloat16)
            return carry

        lax.fori_loop(start, stop, forward_body, 0)

    pass_line(0, far[:1])
    for copy in tunes:
        copy.wait_recv()
    for copy in locals_[4:]:
        copy.wait()
    pass_diag(0, early[:1])
    pass_line(0, far[1:])
    pass_diag(0, early[1:])
    pass_line(1, far[:1])
    normalize(0)
    pass_diag(0, late)
    pass_line(1, far[1:])
    pass_sides(0)
    pass_corner(0)
    pass_diag(1, early)
    arrived(0)
    lay_out(0)
    forward(0, 0, groups // 2)
    pass_diag(1, late)
    pass_sides(1)
    forward(0, groups // 2, groups)
    pass_corner(1)
    normalize(1)
    arrived(1)
    lay_out(1)
    forward(1, 0, groups)

    share = {
        name: reserve(ref.at[other, 0], ref.at[other, 1], partner)
        for name, ref in (("normed", normed), ("acts", acts), ("cots", cots), ("gradpre", gradpre))
    }
    share["acts"].start()
    share["normed"].start()

    statistics(2)

    def head_body(i, carry):
        where = pl.ds(pl.multiple_of(i * rows, rows), rows)
        pred = unit(2, i)
        current = states[0, where, :].astype(jnp.float32)
        fresh = noises[where, :].astype(jnp.float32)
        keep, pull, stir = (coef_ref[j, pl.ds(i, 1), 0:1] for j in range(3))
        squashed = jnp.tanh(keep * current + pull * pred + stir * fresh)
        grad = (1.0 - squashed * squashed) * (reward_ref[...][None] * (pull * loss_scale))
        spread[where, :] = grad
        sums[pl.ds(i, 1), :] = jnp.sum(grad, axis=0, keepdims=True)
        sums[pl.ds(images + i, 1), :] = jnp.sum(grad * pred, axis=0, keepdims=True)
        return carry

    lax.fori_loop(0, images, head_body, 0)

    def pull_back(stage, incoming):
        means_two = group_means(sums[...])
        sums[...] = means_two

        def body(i, carry):
            where = pl.ds(pl.multiple_of(i * rows, rows), rows)
            pulled = scales[stage, pl.ds(i, 1), :] * (
                spread[where, :]
                - sums[pl.ds(i, 1), :]
                - unit(stage, i) * sums[pl.ds(images + i, 1), :]
            )
            if incoming is not None:
                pulled = cots[incoming, 0, where, :].astype(jnp.float32) + pulled
            cots[stage - 1, 0, where, :] = pulled.astype(jnp.bfloat16)
            return carry

        lax.fori_loop(0, images, body, 0)

    pull_back(2, None)

    halves = (late[::-1], early[::-1])
    sides = (qx, qy)
    side_devs = (x_dev, y_dev)
    hop_a, hop_a_size, hop_b, hop_b_size, hop_z, hop_z_size = {}, {}, {}, {}, {}, {}
    for kind in (1, 0):
        for h in range(2):
            for step in range(2):
                hop_a[kind, h, step] = reserve(
                    code_a.at[kind, h, step], in_a.at[kind, h, step], side_devs[h]
                )
            hop_a_size[kind, h] = reserve(
                size_a.at[kind, h], insize_a.at[kind, h], side_devs[h]
            )
            hop_b[kind, h] = reserve(code_b.at[kind, h], in_b.at[kind, h], side_devs[1 - h])
            hop_b_size[kind, h] = reserve(
                size_b.at[kind, h], insize_b.at[kind, h], side_devs[1 - h]
            )
        for j in far:
            hop_z[kind, j] = reserve(code_z.at[kind, j - 1], in_z.at[kind, j - 1], z_dev[j])
            hop_z_size[kind, j] = reserve(
                size_z.at[kind, j - 1], insize_z.at[kind, j - 1], z_dev[j]
            )

    def strip(kind, q, h):
        return jnp.concatenate([grads[kind, q, zj[j]] for j in halves[h]], axis=0)

    def stage_one(kind):
        for h in range(2):
            for step, q in enumerate((qd, sides[h])):
                encode(strip(kind, q, h), code_a.at[kind, h, step], size_a.at[kind, h, step])
            hop_a_size[kind, h].start()
            for step in range(2):
                hop_a[kind, h, step].start()

    def stage_two(kind):
        for h in range(2):
            hop_a_size[kind, h].wait_recv()
            hop_a[kind, h, 0].wait_recv()
            total = strip(kind, sides[1 - h], h) + decode(
                in_a.at[kind, h, 0], insize_a.at[kind, h, 0]
            )
            encode(total, code_b.at[kind, h], size_b.at[kind, h])
            hop_b_size[kind, h].start()
            hop_b[kind, h].start()

    def stage_three(kind):
        for h in range(2):
            hop_a[kind, h, 1].wait_recv()
            hop_b_size[kind, h].wait_recv()
            hop_b[kind, h].wait_recv()
            total = strip(kind, col, h)
            total = total + decode(in_a.at[kind, h, 1], insize_a.at[kind, h, 1])
            total = total + decode(in_b.at[kind, h], insize_b.at[kind, h])
            for place, j in enumerate(halves[h]):
                part = total[place * shard : (place + 1) * shard]
                if j > 0:
                    encode(part, code_z.at[kind, j - 1], size_z.at[kind, j - 1])
                    hop_z_size[kind, j].start()
                    hop_z[kind, j].start()
                else:
                    grads[kind, col, z] = part

    def finish(kind):
        total = grads[kind, col, z]
        for j in far:
            hop_z_size[kind, j].wait_recv()
            hop_z[kind, j].wait_recv()
            total = total + decode(in_z.at[kind, j - 1], insize_z.at[kind, j - 1])
        out_ref[0, :, kind * channels : (kind + 1) * channels] = total

    def weight_grad(section, kind):
        left, right = (normed, gradpre) if kind == 0 else (acts, cots)
        term = contract_rows(
            left[section].reshape(2 * total_rows, channels),
            right[section].reshape(2 * total_rows, channels),
        )
        for owner in range(dp):
            grads[kind, owner % 4, owner // 4] = term[owner * shard : (owner + 1) * shard]

    def grad_preact(section):
        def body(g, carry):
            span = pl.ds(pl.multiple_of(g * joint * rows, rows), joint * rows)
            product = contract_cols(cots[section, 0, span, :], weights[section, 1])
            gradpre[section, 0, span, :] = (product * slopes[section, span, :]).astype(
                jnp.bfloat16
            )
            return carry

        lax.fori_loop(0, groups, body, 0)

    def grad_normed(section):
        gain_row = pbuf[section, 0]

        def body(g, carry):
            span = pl.ds(pl.multiple_of(g * joint * rows, rows), joint * rows)
            product = contract_cols(gradpre[section, 0, span, :], weights[section, 0])
            for j in range(joint):
                i = g * joint + j
                where = pl.ds(pl.multiple_of(i * rows, rows), rows)
                grad = product[j * rows : (j + 1) * rows] * gain_row
                spread[where, :] = grad
                sums[pl.ds(i, 1), :] = jnp.sum(grad, axis=0, keepdims=True)
                sums[pl.ds(images + i, 1), :] = jnp.sum(
                    grad * unit(section, i), axis=0, keepdims=True
                )
            return carry

        lax.fori_loop(0, groups, body, 0)

    def only(which):
        return pl.when(core == which)

    only(0)(share["cots"].start)
    grad_preact(1)
    only(0)(share["gradpre"].start)

    @only(1)
    def _():
        share["acts"].wait_recv()
        share["cots"].wait_recv()
        weight_grad(1, 1)
        stage_one(1)
        share["normed"].wait_recv()
        share["gradpre"].wait_recv()
        weight_grad(1, 0)
        stage_one(0)

    grad_normed(1)

    @only(1)
    def _():
        stage_two(1)

    pull_back(1, 1)
    only(1)(share["cots"].start)
    grad_preact(0)
    only(1)(share["gradpre"].start)

    @only(0)
    def _():
        share["acts"].wait_recv()
        share["cots"].wait_recv()
        weight_grad(0, 1)
        stage_one(1)
        share["normed"].wait_recv()
        share["gradpre"].wait_recv()
        weight_grad(0, 0)
        stage_one(0)
        stage_two(1)

    stage_three(1)
    stage_two(0)
    stage_three(0)
    finish(1)
    finish(0)
    for copy in sent:
        copy.wait_send()


def fused_body(latents, noise, timesteps, reward_dir, gain, time_scale, w_in, w_out):
    dp = lax.axis_size("dp")
    depth = dp // 4
    micro_count = timesteps.shape[0]
    images = micro_count // 2
    rows = latents.shape[0] // micro_count
    channels = latents.shape[1]
    shard = w_in.shape[1]
    loss_scale = 1.0 / math.sqrt(dp * latents.shape[0])
    shape = (dp, depth, shard, channels, images, rows, loss_scale)
    total_rows = images * rows
    strip_rows = depth // 2 * shard
    bf16, f32, i16 = jnp.bfloat16, jnp.float32, jnp.int16
    lines = -(-2 * images // 8) * 8
    square = (shard, channels)
    line = (1, channels)
    copies = 14 * depth + 26
    vmem = pl.BlockSpec(memory_space=pltpu.VMEM)
    codes = [
        pltpu.VMEM((2, 2, 2, strip_rows, channels), i16),
        pltpu.VMEM((2, 2, strip_rows, channels), i16),
        pltpu.VMEM((2, depth - 1) + square, i16),
        pltpu.VMEM((2, 2, 2) + line, f32),
        pltpu.VMEM((2, 2) + line, f32),
        pltpu.VMEM((2, depth - 1) + line, f32),
    ]
    grad_rows = pl.pallas_call(
        functools.partial(step_kernel, shape),
        out_shape=jax.ShapeDtypeStruct((1, shard, 2 * channels), f32),
        in_specs=[vmem] * 4 + [pl.BlockSpec(memory_space=pl.ANY)] * 2
        + [pl.BlockSpec(memory_space=pltpu.SMEM), vmem],
        out_specs=vmem,
        scratch_shapes=[
            pltpu.VMEM((-(-images // 8) * 8, channels), f32),
            pltpu.VMEM((3, -(-images // 8) * 8, 128), f32),
            pltpu.VMEM((2, 2, 4, depth) + square, bf16),
            pltpu.VMEM((2, 2, 1, channels), f32),
            pltpu.VMEM((2, 2, channels, channels), bf16),
            pltpu.VMEM((3, total_rows, channels), bf16),
            pltpu.VMEM((total_rows, channels), bf16),
            pltpu.VMEM((2, 2, total_rows, channels), bf16),
            pltpu.VMEM((2, total_rows, channels), f32),
            pltpu.VMEM((2, 2, total_rows, channels), bf16),
            pltpu.VMEM((2, 2, total_rows, channels), bf16),
            pltpu.VMEM((2, 2, total_rows, channels), bf16),
            pltpu.VMEM((3, lines, channels), f32),
            pltpu.VMEM((3, lines, channels), f32),
            pltpu.VMEM((lines, channels), f32),
            pltpu.VMEM((total_rows, channels), f32),
            pltpu.VMEM((channels, 128), bf16),
            pltpu.VMEM((128, channels), bf16),
            pltpu.VMEM((2, 4, depth) + square, f32),
        ]
        + codes
        + codes
        + [
            pltpu.SemaphoreType.DMA((copies,)),
            pltpu.SemaphoreType.DMA((copies,)),
            pltpu.SemaphoreType.DMA((6,)),
        ],
        compiler_params=pltpu.CompilerParams(
            collective_id=0, has_side_effects=True, vmem_limit_bytes=60 * 1024 * 1024
        ),
    )(w_in, w_out, gain, time_scale, latents, noise, timesteps, reward_dir)
    return grad_rows


def fits(mesh):
    dp = mesh.shape["dp"]
    return mesh.shape["segment"] == 2 and dp >= 16 and dp & (dp - 1) == 0


def solution(mesh):
    placed = (
        P("dp", None),
        P("dp", None),
        P("dp"),
        P(),
        P("segment", None),
        P("segment", None),
        P("segment", "dp", None),
        P("segment", "dp", None),
    )
    return jax.shard_map(
        fused_body if fits(mesh) else body, mesh=mesh, in_specs=placed, out_specs=P("segment", "dp", None), check_vma=False
    )
```

```python
import functools
import math

import jax
import jax.numpy as jnp
from jax import lax
from jax.experimental import pallas as pl
from jax.experimental.pallas import tpu as pltpu
from jax.sharding import PartitionSpec as P

GROUPS = 32
NSTEPS = 1000
STRIDE = 20
LINE = 4
LIMIT = 32760.0
TINY = 1e-30


EPS = 1e-05


def passed_along(shard, axis, by):
    length = lax.axis_size(axis)
    pairs = [(i, i + by) for i in range(length) if 0 <= i + by < length]
    return lax.ppermute(shard, axis, pairs)


def group_norm(state_f32, group_count):
    channels = state_f32.shape[1]
    per_group = channels // group_count
    col_mean = jnp.mean(state_f32, axis=0)
    group_mean = jnp.repeat(jnp.mean(col_mean.reshape(group_count, per_group), axis=1), per_group)
    centered = state_f32 - group_mean
    sq_mean = jnp.mean(centered * centered, axis=0)
    variance = jnp.repeat(jnp.mean(sq_mean.reshape(group_count, per_group), axis=1), per_group)
    return centered * lax.rsqrt(variance + EPS)


def time_embed(timestep, channels):
    half_width = channels // 2
    frequencies = jnp.exp(
        -math.log(10000.0) * jnp.arange(half_width).astype(jnp.float32) / half_width
    )
    phases = timestep.astype(jnp.float32) * frequencies
    return jnp.concatenate([jnp.sin(phases), jnp.cos(phases)])


def alpha_bar(timestep):
    value = ((timestep.astype(jnp.float32) + 1.0) / NSTEPS + 0.008) / 1.008 * (math.pi / 2.0)
    return jnp.cos(value) ** 2


def contract_rows(left, right):
    return lax.dot_general(
        left, right, (((0,), (0,)), ((), ())), preferred_element_type=jnp.float32
    )


def contract_cols(left, right):
    return lax.dot_general(
        left, right, (((1,), (1,)), ((), ())), preferred_element_type=jnp.float32
    )


def block_forward(hidden, gain_row, temb, first, second):
    state_f32 = hidden.astype(jnp.float32)
    normed = (group_norm(state_f32, GROUPS) * gain_row).astype(jnp.bfloat16)
    preact = jnp.dot(normed, first, preferred_element_type=jnp.float32) + temb
    activation = jax.nn.silu(preact).astype(jnp.bfloat16)
    result = (state_f32 + jnp.dot(activation, second, preferred_element_type=jnp.float32)).astype(
        jnp.bfloat16
    )
    return (result, normed, preact, activation)


def block_backward(hidden, gain_row, preact, cotangent, first, second):
    grad_act = contract_cols(cotangent, second)
    gate_value = jax.nn.sigmoid(preact)
    grad_pre = (grad_act * gate_value * (1.0 + preact * (1.0 - gate_value))).astype(jnp.bfloat16)
    grad_norm = contract_cols(grad_pre, first)
    _, pullback = jax.vjp(lambda values: group_norm(values, GROUPS), hidden.astype(jnp.float32))
    new_cot = (cotangent.astype(jnp.float32) + pullback(grad_norm * gain_row)[0]).astype(
        jnp.bfloat16
    )
    return (new_cot, grad_pre)


def weight_term(normed, grad_pre, activation, cotangent):
    return jnp.concatenate(
        [contract_rows(normed, grad_pre), contract_rows(activation, cotangent)], axis=1
    )


def sample_head(hidden, latent, noise_block, timestep, reward_dir, loss_scale):
    ab_now = alpha_bar(timestep)
    ab_prev = alpha_bar(timestep - STRIDE)
    coef_a = jnp.sqrt(ab_now)
    coef_b = jnp.sqrt(1.0 - ab_now)
    coef_p = jnp.sqrt(ab_prev)
    coef_q = jnp.sqrt(0.75 * (1.0 - ab_prev))
    coef_r = 0.5 * jnp.sqrt(1.0 - ab_prev)
    noise_pred, pullback = jax.vjp(
        lambda values: group_norm(values, GROUPS), hidden.astype(jnp.float32)
    )
    current = latent.astype(jnp.float32)
    previous = (
        coef_p * (current - coef_b * noise_pred) / coef_a
        + coef_q * noise_pred
        + coef_r * noise_block.astype(jnp.float32)
    )
    squashed = jnp.tanh(previous)
    grad_pred = (
        (coef_q - coef_p * coef_b / coef_a) * reward_dir * (1.0 - squashed * squashed) * loss_scale
    )
    return pullback(grad_pred)[0].astype(jnp.bfloat16)


def put_slot(buffer, value, slot_index):
    return lax.dynamic_update_index_in_dim(buffer, value, slot_index, 0)


def body(latents, noise, timesteps, reward_dir, gain, time_scale, w_in, w_out):
    segments = lax.axis_size("segment")
    segment_index = lax.axis_index("segment")
    last_segment = segments - 1
    micro_count = timesteps.shape[0]
    crop_rows = latents.shape[0] // micro_count
    channels = latents.shape[1]
    loss_scale = 1.0 / math.sqrt(lax.axis_size("dp") * latents.shape[0])
    tick_count = micro_count + segments - 1
    whole_in, whole_out = (
        lax.all_gather(w_in, "dp", axis=1, tiled=True),
        lax.all_gather(w_out, "dp", axis=1, tiled=True),
    )
    first = whole_in[0]
    second = whole_out[0]
    gain_row = gain[0]
    latent_blocks = latents.reshape(micro_count, crop_rows, channels)
    noise_blocks = noise.reshape(micro_count, crop_rows, channels)
    embeds = jax.vmap(lambda values: time_embed(values, channels))(timesteps) * time_scale[0]
    blank = jnp.zeros((crop_rows, channels), jnp.bfloat16)
    blank_stack = jnp.zeros((micro_count, crop_rows, channels), jnp.bfloat16)
    stored = ()

    def forward_tick(tick_index, state_carry):
        incoming, inputs, head_cots, kept = state_carry
        micro_index = tick_index - segment_index
        active = (micro_index >= 0) & (micro_index < micro_count)
        slot_index = jnp.clip(micro_index, 0, micro_count - 1)
        fresh_input = latent_blocks[slot_index]
        hidden = jnp.where(segment_index == 0, fresh_input, incoming)

        def forward_compute(buffers):
            inputs, head_cots, kept = buffers
            result, normed, preact, activation = block_forward(
                hidden, gain_row, embeds[slot_index], first, second
            )
            inputs = put_slot(inputs, hidden, slot_index)
            head_cot = lax.cond(
                segment_index == last_segment,
                lambda: sample_head(
                    result,
                    fresh_input,
                    noise_blocks[slot_index],
                    timesteps[slot_index],
                    reward_dir,
                    loss_scale,
                ),
                lambda: blank,
            )
            head_cots = put_slot(head_cots, head_cot, slot_index)
            return (result, inputs, head_cots, kept)

        def forward_skipped(buffers):
            return (blank, buffers[0], buffers[1], buffers[2])

        result, inputs, head_cots, kept = lax.cond(
            active, forward_compute, forward_skipped, (inputs, head_cots, kept)
        )
        incoming = passed_along(result, "segment", 1)
        return (incoming, inputs, head_cots, kept)

    _, inputs, head_cots, kept = lax.fori_loop(
        0, tick_count, forward_tick, (blank, blank_stack, blank_stack, stored)
    )
    grad_start = ()
    records = (blank_stack, blank_stack, blank_stack, blank_stack)

    def backward_tick(tick_index, state_carry):
        incoming, grad_sum, records = state_carry
        micro_index = tick_index - (last_segment - segment_index)
        active = (micro_index >= 0) & (micro_index < micro_count)
        slot_index = jnp.clip(micro_index, 0, micro_count - 1)
        cotangent = jnp.where(segment_index == last_segment, head_cots[slot_index], incoming)

        def backward_compute(buffers):
            grad_sum, records = buffers
            hidden = inputs[slot_index]
            _, normed, preact, activation = block_forward(
                hidden, gain_row, embeds[slot_index], first, second
            )
            new_cot, grad_pre = block_backward(hidden, gain_row, preact, cotangent, first, second)
            records = (
                put_slot(records[0], normed, slot_index),
                put_slot(records[1], grad_pre, slot_index),
                put_slot(records[2], activation, slot_index),
                put_slot(records[3], cotangent, slot_index),
            )
            return (new_cot, grad_sum, records)

        def backward_skipped(buffers):
            return (blank, buffers[0], buffers[1])

        result, grad_sum, records = lax.cond(
            active, backward_compute, backward_skipped, (grad_sum, records)
        )
        incoming = passed_along(result, "segment", -1)
        return (incoming, grad_sum, records)

    _, grad_sum, records = lax.fori_loop(0, tick_count, backward_tick, (blank, grad_start, records))
    flat = [buffer.reshape(micro_count * crop_rows, channels) for buffer in records]
    full_terms = weight_term(flat[0], flat[1], flat[2], flat[3])
    grad_rows = lax.psum_scatter(full_terms, "dp", scatter_dimension=0, tiled=True)
    return grad_rows[None]


def split_rows(values):
    high = values.astype(jnp.bfloat16).astype(jnp.float32)
    rest = values - high
    middle = rest.astype(jnp.bfloat16).astype(jnp.float32)
    low = rest - middle
    return jnp.concatenate([high, middle, low], axis=0).astype(jnp.bfloat16)


def encode(block, code_ref, size_ref):
    top = jnp.maximum(jnp.max(jnp.abs(block), axis=0, keepdims=True), TINY)
    size_ref[...] = top * (1.0 / LIMIT)
    code_ref[...] = jnp.round(block * (LIMIT / top)).astype(jnp.int32).astype(jnp.int16)


def decode(code_ref, size_ref):
    return code_ref[...].astype(jnp.int32).astype(jnp.float32) * size_ref[...]


def step_kernel(
    shape,
    win_ref,
    wout_ref,
    gain_ref,
    time_ref,
    latent_ref,
    noise_ref,
    times_ref,
    reward_ref,
    out_ref,
    embed_ref,
    coef_ref,
    wbuf,
    pbuf,
    weights,
    states,
    noises,
    lefts,
    slopes,
    rights,
    means,
    scales,
    sums,
    spread,
    gather_mat,
    scatter_mat,
    grads,
    kept,
    given,
    gift,
    code_a,
    code_b,
    code_z,
    size_a,
    size_b,
    size_z,
    in_a,
    in_b,
    in_z,
    insize_a,
    insize_b,
    insize_z,
    send_sem,
    recv_sem,
    local_sem,
):
    dp, depth, shard, channels, images, rows, loss_scale = shape
    total_rows = images * rows
    me = lax.axis_index("dp")
    core = lax.axis_index("segment")
    other = 1 - core
    col = lax.rem(me, 4)
    z = me // 4
    qx = col + 1 - 2 * lax.rem(col, 2)
    qy = lax.rem(col + 2, 4)
    qd = 3 - col
    x_dev = (z * 4 + qx, core)
    y_dev = (z * 4 + qy, core)
    qu = qx + core * (qy - qx)
    qv = qy + core * (qx - qy)
    u_dev, v_dev = (z * 4 + qu, core), (z * 4 + qv, core)
    partner = (me, other)

    def flipped(j):
        place = z
        bit = 1
        while bit < depth:
            if j & bit:
                place = place + bit * (1 - 2 * lax.rem(z // bit, 2))
            bit *= 2
        return place

    zj = [flipped(j) for j in range(depth)]
    z_dev = [(zj[j] * 4 + col, core) for j in range(depth)]
    far = list(range(1, depth))
    early = list(range(depth // 2))
    late = list(range(depth // 2, depth))
    outgoing, incoming_slots = [0], [0]
    sent = []

    def slots(number):
        first = incoming_slots[0]
        incoming_slots[0] += number
        return first

    def reserve(src, dst, device, slot=None):
        k = outgoing[0]
        outgoing[0] += 1
        copy = pltpu.make_async_remote_copy(
            src_ref=src,
            dst_ref=dst,
            send_sem=send_sem.at[k],
            recv_sem=recv_sem.at[slots(1) if slot is None else slot],
            device_id=device,
            device_id_type=pl.DeviceIdType.MESH,
        )
        sent.append(copy)
        return copy

    base = pl.multiple_of(core * total_rows, total_rows)
    locals_ = [
        pltpu.make_async_copy(source, target, local_sem.at[k])
        for k, (source, target) in enumerate(
            (
                (win_ref.at[0], wbuf.at[core, 0, col, z]),
                (wout_ref.at[0], wbuf.at[core, 1, col, z]),
                (gain_ref, pbuf.at[core, 0]),
                (time_ref, pbuf.at[core, 1]),
                (latent_ref.at[pl.ds(base, total_rows)], states.at[0]),
                (noise_ref.at[pl.ds(base, total_rows)], noises),
            )
        )
    ]
    for copy in locals_:
        copy.start()

    barrier = pltpu.get_barrier_semaphore()
    friends = [x_dev, y_dev, partner] + z_dev[1:]
    for device in friends:
        pl.semaphore_signal(
            barrier, inc=1, device_id=device, device_id_type=pl.DeviceIdType.MESH
        )
    ch = lax.broadcasted_iota(jnp.int32, gather_mat.shape, 0)
    gr = lax.broadcasted_iota(jnp.int32, gather_mat.shape, 1) * (channels // GROUPS)
    inside = (ch >= gr) & (ch < gr + channels // GROUPS)
    gather_mat[...] = jnp.where(inside, 1.0, 0.0).astype(jnp.bfloat16)
    ch = lax.broadcasted_iota(jnp.int32, scatter_mat.shape, 1)
    gr = lax.broadcasted_iota(jnp.int32, scatter_mat.shape, 0) * (channels // GROUPS)
    inside = (ch >= gr) & (ch < gr + channels // GROUPS)
    scatter_mat[...] = jnp.where(inside, 1.0, 0.0).astype(jnp.bfloat16)
    sums[...] = jnp.zeros_like(sums)
    for copy in locals_[:4]:
        copy.wait()
    pl.semaphore_wait(barrier, len(friends))

    def piece(section, q, j):
        return wbuf.at[section, core, q, zj[j]]

    swap = [
        reserve(wbuf.at[core, kind, col, z], wbuf.at[core, kind, col, z], partner)
        for kind in (0, 1)
    ]
    tunes = [
        reserve(gain_ref, pbuf.at[core, 0], partner),
        reserve(time_ref, pbuf.at[core, 1], partner),
    ]
    to_u, to_v, to_z, to_core, to_diag, blocks = {}, {}, {}, {}, {}, {}
    for section in range(2):
        own = piece(section, col, 0)
        for j in range(depth):
            here = piece(section, col, j)
            to_u[section, j] = reserve(here, here, u_dev)
            to_v[section, j] = reserve(here, here, v_dev)
            if j > 0:
                to_core[section, j] = reserve(here, here, partner)
                to_z[section, j] = reserve(own, own, z_dev[j])
            q, device = (qu, v_dev) if j in early else (qv, u_dev)
            passed = piece(section, q, j)
            to_diag[section, j] = reserve(passed, passed, device)
        for q, name in ((qu, "u"), (qv, "v"), (qd, "d")):
            whole = wbuf.at[section, core, q]
            blocks[section, name] = reserve(whole, whole, partner)

    def only(which):
        return pl.when(core == which)

    def own_sides(section):
        to_u[section, 0].start()
        to_v[section, 0].start()

    def own_line(section):
        for j in far:
            to_z[section, j].start()

    def take_swap():
        for copy in swap:
            copy.wait_recv()

    for copy in swap:
        copy.start()

    @only(0)
    def _():
        own_sides(0)
        own_line(0)
        take_swap()
        own_sides(1)
        own_line(1)

    @only(1)
    def _():
        own_sides(1)
        take_swap()
        own_line(0)
        own_sides(0)
        own_line(1)

    for copy in tunes:
        copy.start()

    def pass_line(section, j):
        to_z[section, j].wait_recv()
        to_u[section, j].start()
        to_v[section, j].start()
        to_core[section, j].start()

    def pass_diag(section, j):
        (to_u if j in early else to_v)[section, j].wait_recv()
        to_diag[section, j].start()

    def pass_sides(section):
        for j in late:
            to_u[section, j].wait_recv()
        blocks[section, "u"].start()
        for j in early:
            to_v[section, j].wait_recv()
        blocks[section, "v"].start()

    def pass_corner(section):
        for j in range(depth):
            to_diag[section, j].wait_recv()
        blocks[section, "d"].start()

    def arrived(section):
        for j in far:
            to_core[section, j].wait_recv()
        for name in ("u", "v", "d"):
            blocks[section, name].wait_recv()

    def column(stacked):
        line = lax.broadcasted_iota(jnp.int32, stacked.shape, 0)
        values = jnp.zeros(stacked.shape, jnp.float32)
        for i in range(images):
            values = jnp.where(
                line == i, times_ref[core * images + i].astype(jnp.float32), values
            )
        return values

    def embed_all():
        half_width = channels // 2
        lane = lax.broadcasted_iota(jnp.int32, embed_ref.shape, 1)
        k_index = jnp.where(lane < half_width, lane, lane - half_width).astype(jnp.float32)
        phases = column(embed_ref) * jnp.exp(-math.log(10000.0) * k_index / half_width)
        embed_ref[...] = jnp.where(lane < half_width, jnp.sin(phases), jnp.cos(phases))
        now = column(coef_ref.at[0])
        ab_now, ab_prev = alpha_bar(now), alpha_bar(now - STRIDE)
        coef_a, coef_b = jnp.sqrt(ab_now), jnp.sqrt(1.0 - ab_now)
        coef_p, coef_q = jnp.sqrt(ab_prev), jnp.sqrt(0.75 * (1.0 - ab_prev))
        coef_ref[0] = coef_p / coef_a
        coef_ref[1] = coef_q - coef_p * coef_b / coef_a
        coef_ref[2] = 0.5 * jnp.sqrt(1.0 - ab_prev)

    def group_means(values):
        parts = jnp.dot(
            split_rows(values), gather_mat[...], preferred_element_type=jnp.float32
        )
        lines = values.shape[0]
        total = parts[:lines] + parts[lines : 2 * lines] + parts[2 * lines :]
        total = total * (1.0 / (rows * (channels // GROUPS)))
        parts = jnp.dot(
            split_rows(total), scatter_mat[...], preferred_element_type=jnp.float32
        )
        return parts[:lines] + parts[lines : 2 * lines] + parts[2 * lines :]

    def statistics(stage):
        def mean_body(i, carry):
            block = states[stage, pl.ds(i * rows, rows), :].astype(jnp.float32)
            sums[pl.ds(i, 1), :] = jnp.sum(block, axis=0, keepdims=True)
            return carry

        lax.fori_loop(0, images, mean_body, 0)
        means[stage] = group_means(sums[...])

        def square_body(i, carry):
            block = states[stage, pl.ds(i * rows, rows), :].astype(jnp.float32)
            centered = block - means[stage, pl.ds(i, 1), :]
            sums[pl.ds(i, 1), :] = jnp.sum(centered * centered, axis=0, keepdims=True)
            return carry

        lax.fori_loop(0, images, square_body, 0)
        scales[stage] = lax.rsqrt(group_means(sums[...]) + EPS)

    def unit(stage, i):
        block = states[stage, pl.ds(i * rows, rows), :].astype(jnp.float32)
        return (block - means[stage, pl.ds(i, 1), :]) * scales[stage, pl.ds(i, 1), :]

    def normalize(section):
        statistics(section)
        gain_row = pbuf[section, 0]

        def norm_body(i, carry):
            where = pl.ds(pl.multiple_of(i * rows, rows), rows)
            lefts[0, section, 0, where, :] = (unit(section, i) * gain_row).astype(jnp.bfloat16)
            return carry

        lax.fori_loop(0, images, norm_body, 0)

    def lay_out(section):
        for kind in range(2):
            for pair in range(dp // 2):
                q, zz = (2 * pair) % 4, pair // 2
                both = jnp.concatenate(
                    [
                        wbuf[section, kind, q, zz].astype(jnp.float32),
                        wbuf[section, kind, q + 1, zz].astype(jnp.float32),
                    ],
                    axis=0,
                )
                weights[section, kind, 2 * pair * shard : 2 * (pair + 1) * shard, :] = (
                    both.astype(jnp.bfloat16)
                )

    joint = 2 if images % 2 == 0 else 1
    groups = images // joint

    def forward(section, start, stop):
        time_row = pbuf[section, 1]

        def forward_body(g, carry):
            span = pl.ds(pl.multiple_of(g * joint * rows, rows), joint * rows)
            product = jnp.dot(
                lefts[0, section, 0, span, :],
                weights[section, 0],
                preferred_element_type=jnp.float32,
            )
            for j in range(joint):
                i = g * joint + j
                where = pl.ds(pl.multiple_of(i * rows, rows), rows)
                preact = product[j * rows : (j + 1) * rows] + time_row * embed_ref[pl.ds(i, 1), :]
                gate = jax.nn.sigmoid(preact)
                lefts[1, section, 0, where, :] = (preact * gate).astype(jnp.bfloat16)
                slopes[section, where, :] = gate * (1.0 + preact * (1.0 - gate))
            product = jnp.dot(
                lefts[1, section, 0, span, :],
                weights[section, 1],
                preferred_element_type=jnp.float32,
            )
            states[section + 1, span, :] = (
                states[section, span, :].astype(jnp.float32) + product
            ).astype(jnp.bfloat16)
            return carry

        lax.fori_loop(start, stop, forward_body, 0)

    share_left = [
        reserve(lefts.at[other, section, 0], lefts.at[other, section, 1], partner)
        for section in range(2)
    ]
    share_right = [
        reserve(rights.at[other, section, 0], rights.at[other, section, 1], partner)
        for section in range(2)
    ]
    pass_line(0, 1)
    pass_diag(0, 0)
    pass_line(0, 2)
    pass_line(0, 3)
    pass_diag(0, 1)
    pass_line(1, 1)
    for copy in tunes:
        copy.wait_recv()
    for copy in locals_[4:]:
        copy.wait()
    normalize(0)
    embed_all()
    pass_diag(0, 2)
    pass_diag(0, 3)
    pass_line(1, 2)
    pass_line(1, 3)
    pass_sides(0)
    pass_corner(0)
    pass_diag(1, 0)
    pass_diag(1, 1)
    arrived(0)
    lay_out(0)
    forward(0, 0, groups // 2)
    pass_diag(1, 2)
    pass_diag(1, 3)
    pass_sides(1)
    forward(0, groups // 2, groups)
    share_left[0].start()
    pass_corner(1)
    normalize(1)
    arrived(1)
    lay_out(1)
    forward(1, 0, groups)
    share_left[1].start()

    statistics(2)

    def head_body(i, carry):
        where = pl.ds(pl.multiple_of(i * rows, rows), rows)
        pred = unit(2, i)
        current = states[0, where, :].astype(jnp.float32)
        fresh = noises[where, :].astype(jnp.float32)
        keep, pull, stir = (coef_ref[j, pl.ds(i, 1), 0:1] for j in range(3))
        squashed = jnp.tanh(keep * current + pull * pred + stir * fresh)
        grad = (1.0 - squashed * squashed) * (reward_ref[...][None] * (pull * loss_scale))
        spread[where, :] = grad
        sums[pl.ds(i, 1), :] = jnp.sum(grad, axis=0, keepdims=True)
        sums[pl.ds(images + i, 1), :] = jnp.sum(grad * pred, axis=0, keepdims=True)
        return carry

    lax.fori_loop(0, images, head_body, 0)

    def pull_back(stage, incoming):
        means_two = group_means(sums[...])
        sums[...] = means_two

        def body(i, carry):
            where = pl.ds(pl.multiple_of(i * rows, rows), rows)
            pulled = scales[stage, pl.ds(i, 1), :] * (
                spread[where, :]
                - sums[pl.ds(i, 1), :]
                - unit(stage, i) * sums[pl.ds(images + i, 1), :]
            )
            if incoming is not None:
                pulled = rights[1, incoming, 0, where, :].astype(jnp.float32) + pulled
            rights[1, stage - 1, 0, where, :] = pulled.astype(jnp.bfloat16)
            return carry

        lax.fori_loop(0, images, body, 0)

    pull_back(2, None)

    halves = (late[::-1], early[::-1])
    sides = (qx, qy)
    side_devs = (x_dev, y_dev)
    hop_a, hop_a_size, hop_b, hop_b_size, hop_z, hop_z_size = {}, {}, {}, {}, {}, {}
    z_slots = slots(4 * len(far))
    for section in (1, 0):
        for h in range(2):
            for step in range(2):
                hop_a[section, h, step] = reserve(
                    code_a.at[section, h, step], in_a.at[section, h, step], side_devs[h]
                )
            hop_a_size[section, h] = reserve(
                size_a.at[section, h], insize_a.at[section, h], side_devs[h]
            )
            hop_b[section, h] = reserve(
                code_b.at[section, h], in_b.at[section, h], side_devs[1 - h]
            )
            hop_b_size[section, h] = reserve(
                size_b.at[section, h], insize_b.at[section, h], side_devs[1 - h]
            )
        for j in far:
            slot = z_slots + core * (2 * len(far)) + 2 * (j - 1)
            device = (zj[j] * 4 + col, section)
            hop_z[section, j] = reserve(
                code_z.at[section, j - 1], in_z.at[core, j - 1], device, slot
            )
            hop_z_size[section, j] = reserve(
                size_z.at[section, j - 1], insize_z.at[core, j - 1], device, slot + 1
            )
    hand_over = reserve(given, gift, partner)

    def strip(section, q, h):
        return jnp.concatenate([grads[section, q, zj[j]] for j in halves[h]], axis=0)

    def stage_one(section):
        for h in range(2):
            for step, q in enumerate((qd, sides[h])):
                encode(
                    strip(section, q, h),
                    code_a.at[section, h, step],
                    size_a.at[section, h, step],
                )
            hop_a_size[section, h].start()
            for step in range(2):
                hop_a[section, h, step].start()

    def stage_two(section):
        for h in range(2):
            hop_a_size[section, h].wait_recv()
            hop_a[section, h, 0].wait_recv()
            total = strip(section, sides[1 - h], h) + decode(
                in_a.at[section, h, 0], insize_a.at[section, h, 0]
            )
            encode(total, code_b.at[section, h], size_b.at[section, h])
            hop_b_size[section, h].start()
            hop_b[section, h].start()

    def stage_three(section):
        for h in range(2):
            hop_a[section, h, 1].wait_recv()
            hop_b_size[section, h].wait_recv()
            hop_b[section, h].wait_recv()
            total = strip(section, col, h)
            total = total + decode(in_a.at[section, h, 1], insize_a.at[section, h, 1])
            total = total + decode(in_b.at[section, h], insize_b.at[section, h])
            for place, j in enumerate(halves[h]):
                part = total[place * shard : (place + 1) * shard]
                if j > 0:
                    encode(part, code_z.at[section, j - 1], size_z.at[section, j - 1])
                    hop_z_size[section, j].start()
                    hop_z[section, j].start()
                else:

                    @only(section)
                    def _(part=part):
                        kept[...] = part

                    @only(1 - section)
                    def _(part=part):
                        given[...] = part
                        hand_over.start()

    def finish():
        hand_over.wait_recv()
        for kind in range(2):
            total = jnp.where(core == kind, kept[...], gift[...])
            for j in far:
                slot = z_slots + kind * (2 * len(far)) + 2 * (j - 1)
                for source, target, k in (
                    (size_z, insize_z, slot + 1),
                    (code_z, in_z, slot),
                ):
                    pltpu.make_async_remote_copy(
                        src_ref=source.at[0, j - 1],
                        dst_ref=target.at[kind, j - 1],
                        send_sem=send_sem.at[0],
                        recv_sem=recv_sem.at[k],
                        device_id=z_dev[j],
                        device_id_type=pl.DeviceIdType.MESH,
                    ).wait_recv()
                total = total + decode(in_z.at[kind, j - 1], insize_z.at[kind, j - 1])
            out_ref[0, :, kind * channels : (kind + 1) * channels] = total

    def weight_grad(section):
        term = contract_rows(
            lefts[core, section].reshape(2 * total_rows, channels),
            rights[core, section].reshape(2 * total_rows, channels),
        )
        for owner in range(dp):
            grads[section, owner % 4, owner // 4] = term[owner * shard : (owner + 1) * shard]

    def grad_preact(section):
        def body(g, carry):
            span = pl.ds(pl.multiple_of(g * joint * rows, rows), joint * rows)
            product = contract_cols(rights[1, section, 0, span, :], weights[section, 1])
            rights[0, section, 0, span, :] = (product * slopes[section, span, :]).astype(
                jnp.bfloat16
            )
            return carry

        lax.fori_loop(0, groups, body, 0)

    def grad_normed(section):
        gain_row = pbuf[section, 0]

        def body(g, carry):
            span = pl.ds(pl.multiple_of(g * joint * rows, rows), joint * rows)
            product = contract_cols(rights[0, section, 0, span, :], weights[section, 0])
            for j in range(joint):
                i = g * joint + j
                where = pl.ds(pl.multiple_of(i * rows, rows), rows)
                grad = product[j * rows : (j + 1) * rows] * gain_row
                spread[where, :] = grad
                sums[pl.ds(i, 1), :] = jnp.sum(grad, axis=0, keepdims=True)
                sums[pl.ds(images + i, 1), :] = jnp.sum(
                    grad * unit(section, i), axis=0, keepdims=True
                )
            return carry

        lax.fori_loop(0, groups, body, 0)

    only(0)(share_right[1].start)
    grad_preact(1)
    only(1)(share_right[1].start)
    grad_normed(1)
    share_left[1].wait_recv()
    share_right[1].wait_recv()
    weight_grad(1)
    stage_one(1)
    pull_back(1, 1)
    only(0)(share_right[0].start)
    grad_preact(0)
    only(1)(share_right[0].start)
    stage_two(1)
    share_left[0].wait_recv()
    share_right[0].wait_recv()
    weight_grad(0)
    stage_one(0)
    stage_three(1)
    stage_two(0)
    stage_three(0)
    finish()
    for copy in sent:
        copy.wait_send()


def fused_body(latents, noise, timesteps, reward_dir, gain, time_scale, w_in, w_out):
    dp = lax.axis_size("dp")
    depth = dp // 4
    micro_count = timesteps.shape[0]
    images = micro_count // 2
    rows = latents.shape[0] // micro_count
    channels = latents.shape[1]
    shard = w_in.shape[1]
    loss_scale = 1.0 / math.sqrt(dp * latents.shape[0])
    shape = (dp, depth, shard, channels, images, rows, loss_scale)
    total_rows = images * rows
    strip_rows = depth // 2 * shard
    bf16, f32, i16 = jnp.bfloat16, jnp.float32, jnp.int16
    lines = -(-2 * images // 8) * 8
    square = (shard, channels)
    line = (1, channels)
    far = depth - 1
    copies = 2 * (3 * depth + 2 * far + 3) + 4 * far + 29
    vmem = pl.BlockSpec(memory_space=pltpu.VMEM)
    codes = [
        pltpu.VMEM((2, 2, 2, strip_rows, channels), i16),
        pltpu.VMEM((2, 2, strip_rows, channels), i16),
        pltpu.VMEM((2, depth - 1) + square, i16),
        pltpu.VMEM((2, 2, 2) + line, f32),
        pltpu.VMEM((2, 2) + line, f32),
        pltpu.VMEM((2, depth - 1) + line, f32),
    ]
    grad_rows = pl.pallas_call(
        functools.partial(step_kernel, shape),
        out_shape=jax.ShapeDtypeStruct((1, shard, 2 * channels), f32),
        in_specs=[vmem] * 4 + [pl.BlockSpec(memory_space=pl.ANY)] * 2
        + [pl.BlockSpec(memory_space=pltpu.SMEM), vmem],
        out_specs=vmem,
        scratch_shapes=[
            pltpu.VMEM((-(-images // 8) * 8, channels), f32),
            pltpu.VMEM((3, -(-images // 8) * 8, 128), f32),
            pltpu.VMEM((2, 2, 4, depth) + square, bf16),
            pltpu.VMEM((2, 2, 1, channels), f32),
            pltpu.VMEM((2, 2, channels, channels), bf16),
            pltpu.VMEM((3, total_rows, channels), bf16),
            pltpu.VMEM((total_rows, channels), bf16),
            pltpu.VMEM((2, 2, 2, total_rows, channels), bf16),
            pltpu.VMEM((2, total_rows, channels), f32),
            pltpu.VMEM((2, 2, 2, total_rows, channels), bf16),
            pltpu.VMEM((3, lines, channels), f32),
            pltpu.VMEM((3, lines, channels), f32),
            pltpu.VMEM((lines, channels), f32),
            pltpu.VMEM((total_rows, channels), f32),
            pltpu.VMEM((channels, 128), bf16),
            pltpu.VMEM((128, channels), bf16),
            pltpu.VMEM((2, 4, depth) + square, f32),
            pltpu.VMEM(square, f32),
            pltpu.VMEM(square, f32),
            pltpu.VMEM(square, f32),
        ]
        + codes
        + codes
        + [
            pltpu.SemaphoreType.DMA((copies,)),
            pltpu.SemaphoreType.DMA((copies,)),
            pltpu.SemaphoreType.DMA((6,)),
        ],
        compiler_params=pltpu.CompilerParams(
            collective_id=0, has_side_effects=True, vmem_limit_bytes=60 * 1024 * 1024
        ),
    )(w_in, w_out, gain, time_scale, latents, noise, timesteps, reward_dir)
    return grad_rows


def fits(mesh):
    return mesh.shape["segment"] == 2 and mesh.shape["dp"] == 4 * LINE


def solution(mesh):
    placed = (
        P("dp", None),
        P("dp", None),
        P("dp"),
        P(),
        P("segment", None),
        P("segment", None),
        P("segment", "dp", None),
        P("segment", "dp", None),
    )
    return jax.shard_map(
        fused_body if fits(mesh) else body, mesh=mesh, in_specs=placed, out_specs=P("segment", "dp", None), check_vma=False
    )
```

```python
import functools
import math

import jax
import jax.numpy as jnp
from jax import lax
from jax.experimental import pallas as pl
from jax.experimental.pallas import tpu as pltpu
from jax.sharding import PartitionSpec as P

GROUPS = 32
NSTEPS = 1000
STRIDE = 20
LINE = 4
LIMIT = 32760.0
TINY = 1e-30


EPS = 1e-05


def passed_along(shard, axis, by):
    length = lax.axis_size(axis)
    pairs = [(i, i + by) for i in range(length) if 0 <= i + by < length]
    return lax.ppermute(shard, axis, pairs)


def group_norm(state_f32, group_count):
    channels = state_f32.shape[1]
    per_group = channels // group_count
    col_mean = jnp.mean(state_f32, axis=0)
    group_mean = jnp.repeat(jnp.mean(col_mean.reshape(group_count, per_group), axis=1), per_group)
    centered = state_f32 - group_mean
    sq_mean = jnp.mean(centered * centered, axis=0)
    variance = jnp.repeat(jnp.mean(sq_mean.reshape(group_count, per_group), axis=1), per_group)
    return centered * lax.rsqrt(variance + EPS)


def time_embed(timestep, channels):
    half_width = channels // 2
    frequencies = jnp.exp(
        -math.log(10000.0) * jnp.arange(half_width).astype(jnp.float32) / half_width
    )
    phases = timestep.astype(jnp.float32) * frequencies
    return jnp.concatenate([jnp.sin(phases), jnp.cos(phases)])


def alpha_bar(timestep):
    value = ((timestep.astype(jnp.float32) + 1.0) / NSTEPS + 0.008) / 1.008 * (math.pi / 2.0)
    return jnp.cos(value) ** 2


def contract_rows(left, right):
    return lax.dot_general(
        left, right, (((0,), (0,)), ((), ())), preferred_element_type=jnp.float32
    )


def contract_cols(left, right):
    return lax.dot_general(
        left, right, (((1,), (1,)), ((), ())), preferred_element_type=jnp.float32
    )


def block_forward(hidden, gain_row, temb, first, second):
    state_f32 = hidden.astype(jnp.float32)
    normed = (group_norm(state_f32, GROUPS) * gain_row).astype(jnp.bfloat16)
    preact = jnp.dot(normed, first, preferred_element_type=jnp.float32) + temb
    activation = jax.nn.silu(preact).astype(jnp.bfloat16)
    result = (state_f32 + jnp.dot(activation, second, preferred_element_type=jnp.float32)).astype(
        jnp.bfloat16
    )
    return (result, normed, preact, activation)


def block_backward(hidden, gain_row, preact, cotangent, first, second):
    grad_act = contract_cols(cotangent, second)
    gate_value = jax.nn.sigmoid(preact)
    grad_pre = (grad_act * gate_value * (1.0 + preact * (1.0 - gate_value))).astype(jnp.bfloat16)
    grad_norm = contract_cols(grad_pre, first)
    _, pullback = jax.vjp(lambda values: group_norm(values, GROUPS), hidden.astype(jnp.float32))
    new_cot = (cotangent.astype(jnp.float32) + pullback(grad_norm * gain_row)[0]).astype(
        jnp.bfloat16
    )
    return (new_cot, grad_pre)


def weight_term(normed, grad_pre, activation, cotangent):
    return jnp.concatenate(
        [contract_rows(normed, grad_pre), contract_rows(activation, cotangent)], axis=1
    )


def sample_head(hidden, latent, noise_block, timestep, reward_dir, loss_scale):
    ab_now = alpha_bar(timestep)
    ab_prev = alpha_bar(timestep - STRIDE)
    coef_a = jnp.sqrt(ab_now)
    coef_b = jnp.sqrt(1.0 - ab_now)
    coef_p = jnp.sqrt(ab_prev)
    coef_q = jnp.sqrt(0.75 * (1.0 - ab_prev))
    coef_r = 0.5 * jnp.sqrt(1.0 - ab_prev)
    noise_pred, pullback = jax.vjp(
        lambda values: group_norm(values, GROUPS), hidden.astype(jnp.float32)
    )
    current = latent.astype(jnp.float32)
    previous = (
        coef_p * (current - coef_b * noise_pred) / coef_a
        + coef_q * noise_pred
        + coef_r * noise_block.astype(jnp.float32)
    )
    squashed = jnp.tanh(previous)
    grad_pred = (
        (coef_q - coef_p * coef_b / coef_a) * reward_dir * (1.0 - squashed * squashed) * loss_scale
    )
    return pullback(grad_pred)[0].astype(jnp.bfloat16)


def put_slot(buffer, value, slot_index):
    return lax.dynamic_update_index_in_dim(buffer, value, slot_index, 0)


def body(latents, noise, timesteps, reward_dir, gain, time_scale, w_in, w_out):
    segments = lax.axis_size("segment")
    segment_index = lax.axis_index("segment")
    last_segment = segments - 1
    micro_count = timesteps.shape[0]
    crop_rows = latents.shape[0] // micro_count
    channels = latents.shape[1]
    loss_scale = 1.0 / math.sqrt(lax.axis_size("dp") * latents.shape[0])
    tick_count = micro_count + segments - 1
    whole_in, whole_out = (
        lax.all_gather(w_in, "dp", axis=1, tiled=True),
        lax.all_gather(w_out, "dp", axis=1, tiled=True),
    )
    first = whole_in[0]
    second = whole_out[0]
    gain_row = gain[0]
    latent_blocks = latents.reshape(micro_count, crop_rows, channels)
    noise_blocks = noise.reshape(micro_count, crop_rows, channels)
    embeds = jax.vmap(lambda values: time_embed(values, channels))(timesteps) * time_scale[0]
    blank = jnp.zeros((crop_rows, channels), jnp.bfloat16)
    blank_stack = jnp.zeros((micro_count, crop_rows, channels), jnp.bfloat16)
    stored = ()

    def forward_tick(tick_index, state_carry):
        incoming, inputs, head_cots, kept = state_carry
        micro_index = tick_index - segment_index
        active = (micro_index >= 0) & (micro_index < micro_count)
        slot_index = jnp.clip(micro_index, 0, micro_count - 1)
        fresh_input = latent_blocks[slot_index]
        hidden = jnp.where(segment_index == 0, fresh_input, incoming)

        def forward_compute(buffers):
            inputs, head_cots, kept = buffers
            result, normed, preact, activation = block_forward(
                hidden, gain_row, embeds[slot_index], first, second
            )
            inputs = put_slot(inputs, hidden, slot_index)
            head_cot = lax.cond(
                segment_index == last_segment,
                lambda: sample_head(
                    result,
                    fresh_input,
                    noise_blocks[slot_index],
                    timesteps[slot_index],
                    reward_dir,
                    loss_scale,
                ),
                lambda: blank,
            )
            head_cots = put_slot(head_cots, head_cot, slot_index)
            return (result, inputs, head_cots, kept)

        def forward_skipped(buffers):
            return (blank, buffers[0], buffers[1], buffers[2])

        result, inputs, head_cots, kept = lax.cond(
            active, forward_compute, forward_skipped, (inputs, head_cots, kept)
        )
        incoming = passed_along(result, "segment", 1)
        return (incoming, inputs, head_cots, kept)

    _, inputs, head_cots, kept = lax.fori_loop(
        0, tick_count, forward_tick, (blank, blank_stack, blank_stack, stored)
    )
    grad_start = ()
    records = (blank_stack, blank_stack, blank_stack, blank_stack)

    def backward_tick(tick_index, state_carry):
        incoming, grad_sum, records = state_carry
        micro_index = tick_index - (last_segment - segment_index)
        active = (micro_index >= 0) & (micro_index < micro_count)
        slot_index = jnp.clip(micro_index, 0, micro_count - 1)
        cotangent = jnp.where(segment_index == last_segment, head_cots[slot_index], incoming)

        def backward_compute(buffers):
            grad_sum, records = buffers
            hidden = inputs[slot_index]
            _, normed, preact, activation = block_forward(
                hidden, gain_row, embeds[slot_index], first, second
            )
            new_cot, grad_pre = block_backward(hidden, gain_row, preact, cotangent, first, second)
            records = (
                put_slot(records[0], normed, slot_index),
                put_slot(records[1], grad_pre, slot_index),
                put_slot(records[2], activation, slot_index),
                put_slot(records[3], cotangent, slot_index),
            )
            return (new_cot, grad_sum, records)

        def backward_skipped(buffers):
            return (blank, buffers[0], buffers[1])

        result, grad_sum, records = lax.cond(
            active, backward_compute, backward_skipped, (grad_sum, records)
        )
        incoming = passed_along(result, "segment", -1)
        return (incoming, grad_sum, records)

    _, grad_sum, records = lax.fori_loop(0, tick_count, backward_tick, (blank, grad_start, records))
    flat = [buffer.reshape(micro_count * crop_rows, channels) for buffer in records]
    full_terms = weight_term(flat[0], flat[1], flat[2], flat[3])
    grad_rows = lax.psum_scatter(full_terms, "dp", scatter_dimension=0, tiled=True)
    return grad_rows[None]


def split_rows(values):
    high = values.astype(jnp.bfloat16).astype(jnp.float32)
    rest = values - high
    middle = rest.astype(jnp.bfloat16).astype(jnp.float32)
    low = rest - middle
    return jnp.concatenate([high, middle, low], axis=0).astype(jnp.bfloat16)


def encode(block, code_ref, size_ref):
    top = jnp.maximum(jnp.max(jnp.abs(block), axis=0, keepdims=True), TINY)
    size_ref[...] = top * (1.0 / LIMIT)
    code_ref[...] = jnp.round(block * (LIMIT / top)).astype(jnp.int32).astype(jnp.int16)


def decode(code_ref, size_ref):
    return code_ref[...].astype(jnp.int32).astype(jnp.float32) * size_ref[...]


def step_kernel(
    shape,
    win_ref,
    wout_ref,
    gain_ref,
    time_ref,
    latent_ref,
    noise_ref,
    times_in,
    reward_in,
    out_ref,
    times_ref,
    reward_ref,
    embed_ref,
    coef_ref,
    wbuf,
    pbuf,
    weights,
    states,
    noises,
    lefts,
    slopes,
    rights,
    means,
    scales,
    sums,
    spread,
    gather_mat,
    scatter_mat,
    grads,
    kept,
    given,
    gift,
    code_a,
    code_b,
    code_z,
    size_a,
    size_b,
    size_z,
    in_a,
    in_b,
    in_z,
    insize_a,
    insize_b,
    insize_z,
    send_sem,
    recv_sem,
    local_sem,
):
    dp, depth, shard, channels, images, rows, loss_scale = shape
    total_rows = images * rows
    me = lax.axis_index("dp")
    core = lax.axis_index("segment")
    other = 1 - core
    col = lax.rem(me, 4)
    z = me // 4
    qx = col + 1 - 2 * lax.rem(col, 2)
    qy = lax.rem(col + 2, 4)
    qd = 3 - col
    x_dev = (z * 4 + qx, core)
    y_dev = (z * 4 + qy, core)
    qu = qx + core * (qy - qx)
    qv = qy + core * (qx - qy)
    u_dev, v_dev = (z * 4 + qu, core), (z * 4 + qv, core)
    partner = (me, other)

    def flipped(j):
        place = z
        bit = 1
        while bit < depth:
            if j & bit:
                place = place + bit * (1 - 2 * lax.rem(z // bit, 2))
            bit *= 2
        return place

    zj = [flipped(j) for j in range(depth)]
    z_dev = [(zj[j] * 4 + col, core) for j in range(depth)]
    far = list(range(1, depth))
    early = list(range(depth // 2))
    late = list(range(depth // 2, depth))
    outgoing, incoming_slots = [0], [0]
    sent = []

    def slots(number):
        first = incoming_slots[0]
        incoming_slots[0] += number
        return first

    def reserve(src, dst, device, slot=None):
        k = outgoing[0]
        outgoing[0] += 1
        copy = pltpu.make_async_remote_copy(
            src_ref=src,
            dst_ref=dst,
            send_sem=send_sem.at[k],
            recv_sem=recv_sem.at[slots(1) if slot is None else slot],
            device_id=device,
            device_id_type=pl.DeviceIdType.MESH,
        )
        sent.append(copy)
        return copy

    base = pl.multiple_of(core * total_rows, total_rows)
    locals_ = [
        pltpu.make_async_copy(source, target, local_sem.at[k])
        for k, (source, target) in enumerate(
            (
                (win_ref.at[0], wbuf.at[core, 0, col, z]),
                (wout_ref.at[0], wbuf.at[core, 1, col, z]),
                (gain_ref, pbuf.at[core, 0]),
                (time_ref, pbuf.at[core, 1]),
                (latent_ref.at[pl.ds(base, total_rows)], states.at[0]),
                (noise_ref.at[pl.ds(base, total_rows)], noises),
                (times_in, times_ref),
                (reward_in, reward_ref),
            )
        )
    ]
    for copy in locals_:
        copy.start()

    barrier = pltpu.get_barrier_semaphore()
    friends = [x_dev, y_dev, partner] + z_dev[1:]
    for device in friends:
        pl.semaphore_signal(
            barrier, inc=1, device_id=device, device_id_type=pl.DeviceIdType.MESH
        )
    ch = lax.broadcasted_iota(jnp.int32, gather_mat.shape, 0)
    gr = lax.broadcasted_iota(jnp.int32, gather_mat.shape, 1) * (channels // GROUPS)
    inside = (ch >= gr) & (ch < gr + channels // GROUPS)
    gather_mat[...] = jnp.where(inside, 1.0, 0.0).astype(jnp.bfloat16)
    ch = lax.broadcasted_iota(jnp.int32, scatter_mat.shape, 1)
    gr = lax.broadcasted_iota(jnp.int32, scatter_mat.shape, 0) * (channels // GROUPS)
    inside = (ch >= gr) & (ch < gr + channels // GROUPS)
    scatter_mat[...] = jnp.where(inside, 1.0, 0.0).astype(jnp.bfloat16)
    sums[...] = jnp.zeros_like(sums)
    for copy in locals_[:4]:
        copy.wait()
    pl.semaphore_wait(barrier, len(friends))

    def piece(section, q, j):
        return wbuf.at[section, core, q, zj[j]]

    swap = [
        reserve(wbuf.at[core, kind, col, z], wbuf.at[core, kind, col, z], partner)
        for kind in (0, 1)
    ]
    tunes = [
        reserve(pbuf.at[core, 0], pbuf.at[core, 0], partner),
        reserve(pbuf.at[core, 1], pbuf.at[core, 1], partner),
    ]
    to_u, to_v, to_z, to_core, to_diag, blocks = {}, {}, {}, {}, {}, {}
    for section in range(2):
        own = piece(section, col, 0)
        for j in range(depth):
            here = piece(section, col, j)
            to_u[section, j] = reserve(here, here, u_dev)
            to_v[section, j] = reserve(here, here, v_dev)
            if j > 0:
                to_core[section, j] = reserve(here, here, partner)
                to_z[section, j] = reserve(own, own, z_dev[j])
            q, device = (qu, v_dev) if j in early else (qv, u_dev)
            passed = piece(section, q, j)
            to_diag[section, j] = reserve(passed, passed, device)
        for q, name in ((qu, "u"), (qv, "v"), (qd, "d")):
            whole = wbuf.at[section, core, q]
            blocks[section, name] = reserve(whole, whole, partner)

    def only(which):
        return pl.when(core == which)

    def own_sides(section):
        to_u[section, 0].start()
        to_v[section, 0].start()

    def own_line(section):
        for j in far:
            to_z[section, j].start()

    def take_swap():
        for copy in swap:
            copy.wait_recv()

    for copy in swap:
        copy.start()

    @only(0)
    def _():
        own_sides(0)
        own_line(0)
        take_swap()
        own_sides(1)
        own_line(1)

    @only(1)
    def _():
        own_sides(1)
        take_swap()
        own_line(0)
        own_sides(0)
        own_line(1)

    for copy in tunes:
        copy.start()

    def pass_line(section, j):
        to_z[section, j].wait_recv()
        to_u[section, j].start()
        to_v[section, j].start()
        to_core[section, j].start()

    def pass_diag(section, j):
        (to_u if j in early else to_v)[section, j].wait_recv()
        to_diag[section, j].start()

    def pass_sides(section):
        for j in late:
            to_u[section, j].wait_recv()
        blocks[section, "u"].start()
        for j in early:
            to_v[section, j].wait_recv()
        blocks[section, "v"].start()

    def pass_corner(section):
        for j in range(depth):
            to_diag[section, j].wait_recv()
        blocks[section, "d"].start()

    def arrived(section):
        for j in far:
            to_core[section, j].wait_recv()
        for name in ("u", "v", "d"):
            blocks[section, name].wait_recv()

    def column(stacked):
        line = lax.broadcasted_iota(jnp.int32, stacked.shape, 0)
        values = jnp.zeros(stacked.shape, jnp.float32)
        for i in range(images):
            values = jnp.where(
                line == i, times_ref[core * images + i].astype(jnp.float32), values
            )
        return values

    def embed_all():
        half_width = channels // 2
        lane = lax.broadcasted_iota(jnp.int32, embed_ref.shape, 1)
        k_index = jnp.where(lane < half_width, lane, lane - half_width).astype(jnp.float32)
        phases = column(embed_ref) * jnp.exp(-math.log(10000.0) * k_index / half_width)
        embed_ref[...] = jnp.where(lane < half_width, jnp.sin(phases), jnp.cos(phases))
        now = column(coef_ref.at[0])
        ab_now, ab_prev = alpha_bar(now), alpha_bar(now - STRIDE)
        coef_a, coef_b = jnp.sqrt(ab_now), jnp.sqrt(1.0 - ab_now)
        coef_p, coef_q = jnp.sqrt(ab_prev), jnp.sqrt(0.75 * (1.0 - ab_prev))
        coef_ref[0] = coef_p / coef_a
        coef_ref[1] = coef_q - coef_p * coef_b / coef_a
        coef_ref[2] = 0.5 * jnp.sqrt(1.0 - ab_prev)

    def group_means(values):
        parts = jnp.dot(
            split_rows(values), gather_mat[...], preferred_element_type=jnp.float32
        )
        lines = values.shape[0]
        total = parts[:lines] + parts[lines : 2 * lines] + parts[2 * lines :]
        total = total * (1.0 / (rows * (channels // GROUPS)))
        parts = jnp.dot(
            split_rows(total), scatter_mat[...], preferred_element_type=jnp.float32
        )
        return parts[:lines] + parts[lines : 2 * lines] + parts[2 * lines :]

    def statistics(stage):
        def mean_body(i, carry):
            block = states[stage, pl.ds(i * rows, rows), :].astype(jnp.float32)
            sums[pl.ds(i, 1), :] = jnp.sum(block, axis=0, keepdims=True)
            return carry

        lax.fori_loop(0, images, mean_body, 0)
        means[stage] = group_means(sums[...])

        def square_body(i, carry):
            block = states[stage, pl.ds(i * rows, rows), :].astype(jnp.float32)
            centered = block - means[stage, pl.ds(i, 1), :]
            sums[pl.ds(i, 1), :] = jnp.sum(centered * centered, axis=0, keepdims=True)
            return carry

        lax.fori_loop(0, images, square_body, 0)
        scales[stage] = lax.rsqrt(group_means(sums[...]) + EPS)

    def unit(stage, i):
        block = states[stage, pl.ds(i * rows, rows), :].astype(jnp.float32)
        return (block - means[stage, pl.ds(i, 1), :]) * scales[stage, pl.ds(i, 1), :]

    def normalize(section):
        statistics(section)
        gain_row = pbuf[section, 0]

        def norm_body(i, carry):
            where = pl.ds(pl.multiple_of(i * rows, rows), rows)
            lefts[0, section, 0, where, :] = (unit(section, i) * gain_row).astype(jnp.bfloat16)
            return carry

        lax.fori_loop(0, images, norm_body, 0)

    def lay_out(section):
        for kind in range(2):
            for pair in range(dp // 2):
                q, zz = (2 * pair) % 4, pair // 2
                both = jnp.concatenate(
                    [
                        wbuf[section, kind, q, zz].astype(jnp.float32),
                        wbuf[section, kind, q + 1, zz].astype(jnp.float32),
                    ],
                    axis=0,
                )
                weights[section, kind, 2 * pair * shard : 2 * (pair + 1) * shard, :] = (
                    both.astype(jnp.bfloat16)
                )

    joint = next(n for n in (4, 2, 1) if images % n == 0)
    groups = images // joint

    def forward(section, start, stop):
        time_row = pbuf[section, 1]

        def forward_body(g, carry):
            span = pl.ds(pl.multiple_of(g * joint * rows, rows), joint * rows)
            product = jnp.dot(
                lefts[0, section, 0, span, :],
                weights[section, 0],
                preferred_element_type=jnp.float32,
            )
            for j in range(joint):
                i = g * joint + j
                where = pl.ds(pl.multiple_of(i * rows, rows), rows)
                preact = product[j * rows : (j + 1) * rows] + time_row * embed_ref[pl.ds(i, 1), :]
                gate = jax.nn.sigmoid(preact)
                lefts[1, section, 0, where, :] = (preact * gate).astype(jnp.bfloat16)
                slopes[section, where, :] = gate * (1.0 + preact * (1.0 - gate))
            product = jnp.dot(
                lefts[1, section, 0, span, :],
                weights[section, 1],
                preferred_element_type=jnp.float32,
            )
            states[section + 1, span, :] = (
                states[section, span, :].astype(jnp.float32) + product
            ).astype(jnp.bfloat16)
            return carry

        lax.fori_loop(start, stop, forward_body, 0)

    gathers = list(sent)
    del sent[:]
    share_left = [
        reserve(lefts.at[other, section, 0], lefts.at[other, section, 1], partner)
        for section in range(2)
    ]
    share_right = [
        reserve(rights.at[other, section, 0], rights.at[other, section, 1], partner)
        for section in range(2)
    ]
    pass_line(0, 1)
    pass_diag(0, 0)
    pass_line(0, 2)
    pass_line(0, 3)
    pass_diag(0, 1)
    pass_line(1, 1)
    for copy in tunes:
        copy.wait_recv()
    for copy in locals_[4:]:
        copy.wait()
    normalize(0)
    embed_all()
    pass_diag(0, 2)
    pass_diag(0, 3)
    pass_line(1, 2)
    pass_line(1, 3)
    pass_sides(0)
    pass_corner(0)
    pass_diag(1, 0)
    pass_diag(1, 1)
    arrived(0)
    lay_out(0)
    forward(0, 0, groups // 2)
    pass_diag(1, 2)
    pass_diag(1, 3)
    pass_sides(1)
    forward(0, groups // 2, groups)
    share_left[0].start()
    pass_corner(1)
    normalize(1)
    arrived(1)
    lay_out(1)
    forward(1, 0, groups)
    share_left[1].start()

    statistics(2)

    def head_body(i, carry):
        where = pl.ds(pl.multiple_of(i * rows, rows), rows)
        pred = unit(2, i)
        current = states[0, where, :].astype(jnp.float32)
        fresh = noises[where, :].astype(jnp.float32)
        keep, pull, stir = (coef_ref[j, pl.ds(i, 1), 0:1] for j in range(3))
        squashed = jnp.tanh(keep * current + pull * pred + stir * fresh)
        grad = (1.0 - squashed * squashed) * (reward_ref[...][None] * (pull * loss_scale))
        spread[where, :] = grad
        sums[pl.ds(i, 1), :] = jnp.sum(grad, axis=0, keepdims=True)
        sums[pl.ds(images + i, 1), :] = jnp.sum(grad * pred, axis=0, keepdims=True)
        return carry

    lax.fori_loop(0, images, head_body, 0)

    def pull_back(stage, incoming):
        means_two = group_means(sums[...])
        sums[...] = means_two

        def body(i, carry):
            where = pl.ds(pl.multiple_of(i * rows, rows), rows)
            pulled = scales[stage, pl.ds(i, 1), :] * (
                spread[where, :]
                - sums[pl.ds(i, 1), :]
                - unit(stage, i) * sums[pl.ds(images + i, 1), :]
            )
            if incoming is not None:
                pulled = rights[1, incoming, 0, where, :].astype(jnp.float32) + pulled
            rights[1, stage - 1, 0, where, :] = pulled.astype(jnp.bfloat16)
            return carry

        lax.fori_loop(0, images, body, 0)

    pull_back(2, None)

    for copy in gathers:
        copy.wait_send()
    outgoing[0] = 0
    halves = (late[::-1], early[::-1])
    sides = (qx, qy)
    side_devs = (x_dev, y_dev)
    hop_a, hop_a_size, hop_b, hop_b_size, hop_z, hop_z_size = {}, {}, {}, {}, {}, {}
    z_slots = slots(4 * len(far))
    for section in (1, 0):
        for h in range(2):
            for step in range(2):
                hop_a[section, h, step] = reserve(
                    code_a.at[section, h, step], in_a.at[section, h, step], side_devs[h]
                )
            hop_a_size[section, h] = reserve(
                size_a.at[section, h], insize_a.at[section, h], side_devs[h]
            )
            hop_b[section, h] = reserve(
                code_b.at[section, h], in_b.at[section, h], side_devs[1 - h]
            )
            hop_b_size[section, h] = reserve(
                size_b.at[section, h], insize_b.at[section, h], side_devs[1 - h]
            )
        for j in far:
            slot = z_slots + core * (2 * len(far)) + 2 * (j - 1)
            device = (zj[j] * 4 + col, section)
            hop_z[section, j] = reserve(
                code_z.at[section, j - 1], in_z.at[core, j - 1], device, slot
            )
            hop_z_size[section, j] = reserve(
                size_z.at[section, j - 1], insize_z.at[core, j - 1], device, slot + 1
            )
    hand_over = reserve(given, gift, partner)

    def strip(section, q, h):
        return jnp.concatenate([grads[section, q, zj[j]] for j in halves[h]], axis=0)

    def stage_one(section):
        for h in range(2):
            for step, q in enumerate((qd, sides[h])):
                encode(
                    strip(section, q, h),
                    code_a.at[section, h, step],
                    size_a.at[section, h, step],
                )
            hop_a_size[section, h].start()
            for step in range(2):
                hop_a[section, h, step].start()

    def stage_two(section):
        for h in range(2):
            hop_a_size[section, h].wait_recv()
            hop_a[section, h, 0].wait_recv()
            total = strip(section, sides[1 - h], h) + decode(
                in_a.at[section, h, 0], insize_a.at[section, h, 0]
            )
            encode(total, code_b.at[section, h], size_b.at[section, h])
            hop_b_size[section, h].start()
            hop_b[section, h].start()

    def stage_three(section):
        for h in range(2):
            hop_a[section, h, 1].wait_recv()
            hop_b_size[section, h].wait_recv()
            hop_b[section, h].wait_recv()
            total = strip(section, col, h)
            total = total + decode(in_a.at[section, h, 1], insize_a.at[section, h, 1])
            total = total + decode(in_b.at[section, h], insize_b.at[section, h])
            for place, j in enumerate(halves[h]):
                part = total[place * shard : (place + 1) * shard]
                if j > 0:
                    encode(part, code_z.at[section, j - 1], size_z.at[section, j - 1])
                    hop_z_size[section, j].start()
                    hop_z[section, j].start()
                else:

                    @only(section)
                    def _(part=part):
                        kept[...] = part

                    @only(1 - section)
                    def _(part=part):
                        given[...] = part
                        hand_over.start()

    def finish():
        hand_over.wait_recv()
        for kind in range(2):
            total = jnp.where(core == kind, kept[...], gift[...])
            for j in far:
                slot = z_slots + kind * (2 * len(far)) + 2 * (j - 1)
                for source, target, k in (
                    (size_z, insize_z, slot + 1),
                    (code_z, in_z, slot),
                ):
                    pltpu.make_async_remote_copy(
                        src_ref=source.at[0, j - 1],
                        dst_ref=target.at[kind, j - 1],
                        send_sem=send_sem.at[0],
                        recv_sem=recv_sem.at[k],
                        device_id=z_dev[j],
                        device_id_type=pl.DeviceIdType.MESH,
                    ).wait_recv()
                total = total + decode(in_z.at[kind, j - 1], insize_z.at[kind, j - 1])
            out_ref[0, :, kind * channels : (kind + 1) * channels] = total

    def weight_grad(section):
        term = contract_rows(
            lefts[core, section].reshape(2 * total_rows, channels),
            rights[core, section].reshape(2 * total_rows, channels),
        )
        for owner in range(dp):
            grads[section, owner % 4, owner // 4] = term[owner * shard : (owner + 1) * shard]

    def grad_preact(section):
        def body(g, carry):
            span = pl.ds(pl.multiple_of(g * joint * rows, rows), joint * rows)
            product = contract_cols(rights[1, section, 0, span, :], weights[section, 1])
            rights[0, section, 0, span, :] = (product * slopes[section, span, :]).astype(
                jnp.bfloat16
            )
            return carry

        lax.fori_loop(0, groups, body, 0)

    def grad_normed(section):
        gain_row = pbuf[section, 0]

        def body(g, carry):
            span = pl.ds(pl.multiple_of(g * joint * rows, rows), joint * rows)
            product = contract_cols(rights[0, section, 0, span, :], weights[section, 0])
            for j in range(joint):
                i = g * joint + j
                where = pl.ds(pl.multiple_of(i * rows, rows), rows)
                grad = product[j * rows : (j + 1) * rows] * gain_row
                spread[where, :] = grad
                sums[pl.ds(i, 1), :] = jnp.sum(grad, axis=0, keepdims=True)
                sums[pl.ds(images + i, 1), :] = jnp.sum(
                    grad * unit(section, i), axis=0, keepdims=True
                )
            return carry

        lax.fori_loop(0, groups, body, 0)

    only(0)(share_right[1].start)
    grad_preact(1)
    only(1)(share_right[1].start)
    grad_normed(1)
    share_left[1].wait_recv()
    share_right[1].wait_recv()
    weight_grad(1)
    stage_one(1)
    pull_back(1, 1)
    only(0)(share_right[0].start)
    grad_preact(0)
    only(1)(share_right[0].start)
    stage_two(1)
    share_left[0].wait_recv()
    share_right[0].wait_recv()
    weight_grad(0)
    stage_one(0)
    stage_three(1)
    stage_two(0)
    stage_three(0)
    finish()
    for copy in sent:
        copy.wait_send()


def fused_body(latents, noise, timesteps, reward_dir, gain, time_scale, w_in, w_out):
    dp = lax.axis_size("dp")
    depth = dp // 4
    micro_count = timesteps.shape[0]
    images = micro_count // 2
    rows = latents.shape[0] // micro_count
    channels = latents.shape[1]
    shard = w_in.shape[1]
    loss_scale = 1.0 / math.sqrt(dp * latents.shape[0])
    shape = (dp, depth, shard, channels, images, rows, loss_scale)
    total_rows = images * rows
    strip_rows = depth // 2 * shard
    bf16, f32, i16 = jnp.bfloat16, jnp.float32, jnp.int16
    lines = -(-2 * images // 8) * 8
    square = (shard, channels)
    line = (1, channels)
    far = depth - 1
    copies = 2 * (3 * depth + 2 * far + 3) + 4 * far + 29
    vmem = pl.BlockSpec(memory_space=pltpu.VMEM)
    codes = [
        pltpu.VMEM((2, 2, 2, strip_rows, channels), i16),
        pltpu.VMEM((2, 2, strip_rows, channels), i16),
        pltpu.VMEM((2, depth - 1) + square, i16),
        pltpu.VMEM((2, 2, 2) + line, f32),
        pltpu.VMEM((2, 2) + line, f32),
        pltpu.VMEM((2, depth - 1) + line, f32),
    ]
    grad_rows = pl.pallas_call(
        functools.partial(step_kernel, shape),
        out_shape=jax.ShapeDtypeStruct((1, shard, 2 * channels), f32),
        in_specs=[pl.BlockSpec(memory_space=pl.ANY)] * 8,
        out_specs=vmem,
        scratch_shapes=[
            pltpu.SMEM((micro_count,), jnp.int32),
            pltpu.VMEM((channels,), f32),
            pltpu.VMEM((-(-images // 8) * 8, channels), f32),
            pltpu.VMEM((3, -(-images // 8) * 8, 128), f32),
            pltpu.VMEM((2, 2, 4, depth) + square, bf16),
            pltpu.VMEM((2, 2, 1, channels), f32),
            pltpu.VMEM((2, 2, channels, channels), bf16),
            pltpu.VMEM((3, total_rows, channels), bf16),
            pltpu.VMEM((total_rows, channels), bf16),
            pltpu.VMEM((2, 2, 2, total_rows, channels), bf16),
            pltpu.VMEM((2, total_rows, channels), f32),
            pltpu.VMEM((2, 2, 2, total_rows, channels), bf16),
            pltpu.VMEM((3, lines, channels), f32),
            pltpu.VMEM((3, lines, channels), f32),
            pltpu.VMEM((lines, channels), f32),
            pltpu.VMEM((total_rows, channels), f32),
            pltpu.VMEM((channels, 128), bf16),
            pltpu.VMEM((128, channels), bf16),
            pltpu.VMEM((2, 4, depth) + square, f32),
            pltpu.VMEM(square, f32),
            pltpu.VMEM(square, f32),
            pltpu.VMEM(square, f32),
        ]
        + codes
        + codes
        + [
            pltpu.SemaphoreType.DMA((copies - 4 * far - 21,)),
            pltpu.SemaphoreType.DMA((copies,)),
            pltpu.SemaphoreType.DMA((8,)),
        ],
        compiler_params=pltpu.CompilerParams(
            collective_id=0, has_side_effects=True, vmem_limit_bytes=60 * 1024 * 1024
        ),
    )(w_in, w_out, gain, time_scale, latents, noise, timesteps, reward_dir)
    return grad_rows


def fits(mesh):
    return mesh.shape["segment"] == 2 and mesh.shape["dp"] == 4 * LINE


def solution(mesh):
    placed = (
        P("dp", None),
        P("dp", None),
        P("dp"),
        P(),
        P("segment", None),
        P("segment", None),
        P("segment", "dp", None),
        P("segment", "dp", None),
    )
    return jax.shard_map(
        fused_body if fits(mesh) else body, mesh=mesh, in_specs=placed, out_specs=P("segment", "dp", None), check_vma=False
    )
```
